32 devices in a mesh: group: 2 (over x), row: 16 (over z, y, core).
Axes of the slice: x: 2, y: 2, z: 4, core: 2. Of those that a mesh axis runs over, the one named last changes fastest.
Arguments:
- features: bfloat16 [256, 128, 384], P(('group', 'row')), parts along dimension 0, may hold values from -6 to 6
- qkv_weight: bfloat16 [384, 1152], replicated, may hold values from -0.5 to 0.5
- grad_output: bfloat16 [256, 128, 384], P(('group', 'row')), parts along dimension 0, may hold values from -6 to 6
Outputs:
- grad_features: bfloat16 [256, 128, 384], P(('group', 'row')), parts along dimension 0
- grad_weight: float32 [768, 1152], P(('group', 'row')), parts along dimension 0
The draws below stay inside these ranges and needn't reach their ends.
There are 2 independent parts, one for each index of `group`. The reference program is written for one: setup_inputs(seed, part) draws one part's arguments, and reference() takes and returns one part's arrays. A program takes and returns all parts, laid end to end along the dimension named above; an argument that names none is the same for every part. Nothing has to cross between parts.
All inputs are finite; a program needn't handle non-finite values.
Results may differ from the reference program's by a relative error of at most 0.012.
The reference program's roundings to bfloat16 on the way count: a program that leaves them out, or rounds other values in their place, can miss the bound.
Values may be sent and summed in bfloat16 or wider, within the bound.
No kernel may reach another device: no remote copies, remote signals or barrier semaphores. Data moves between devices by JAX's collectives and lax.ppermute only.
A program may use at most 128 MiB of HBM per device.

```python
import math
import jax
import jax.numpy as jnp
from jax import lax

D = 384
HEADS = 12
WINDOW = 7
DILATION = 2
ROWS_DEV = 8
COLS = 128
H = 128
N_ROW = 16


def draw_features(key, part):
    noise_key = jax.random.fold_in(key, 101)
    keys = jax.random.split(noise_key, 1)
    drawn = jnp.clip(jax.random.normal(keys[0], (H, COLS, D), jnp.float32), -6.0, 6.0)
    return drawn.astype(jnp.bfloat16)


def draw_qkv_weight(key, part):
    weight_key = jax.random.fold_in(key, 202)
    scale = D ** (-0.5)
    weight = jnp.clip(jax.random.normal(weight_key, (D, 3 * D), jnp.float32) * scale, -0.5, 0.5)
    return weight.astype(jnp.bfloat16)


def block_scale(stream_key, shape, cuts, smallest, largest):
    gain, own = 1.0, jax.random.fold_in(stream_key, 6)
    for dim, blocks in cuts:
        heights = jnp.exp(jax.random.uniform(jax.random.fold_in(own, dim), (blocks,), jnp.float32, smallest / len(cuts), largest / len(cuts)))
        gain = gain * jnp.repeat(heights, shape[dim] // blocks).reshape([-1 if axis == dim else 1 for axis in range(len(shape))])
    return gain


def scatter_about(key, shape, scale, reach, cuts=(), kind=jnp.bfloat16):
    values = jax.random.normal(key, shape, jnp.float32) * scale
    if len(cuts) > 0:
        values = block_scale(key, shape, cuts, -0.22, 0.18) * values
    return jnp.clip(values, min=-reach, max=reach).astype(kind)


def setup_inputs(seed: int = 0, part: int = 0) -> dict:
    streams_of = jax.random.split(jax.random.key(seed), 4)
    own_keys = jax.random.split(jax.random.fold_in(streams_of[3], part), 4)
    return {
        "features": draw_features(jax.random.fold_in(jax.random.fold_in(streams_of[3], part), 71), part),
        "qkv_weight": draw_qkv_weight(jax.random.fold_in(streams_of[3], 71), part),
        "grad_output": scatter_about(own_keys[2], (H, COLS, D), 1.0, 6.0, ((0, 16),)),
    }


def window_pairs():
    return [(a, b) for a in range(WINDOW) for b in range(WINDOW)]


def inside(first_row, row_count, col_count, total_rows, row_shift, col_shift):
    row_ids = first_row + jnp.arange(row_count, dtype=jnp.int32) + row_shift
    col_ids = jnp.arange(col_count, dtype=jnp.int32) + col_shift
    row_good = (row_ids >= 0) & (row_ids < total_rows)
    col_good = (col_ids >= 0) & (col_ids < col_count)
    return row_good[:, None] & col_good[None, :]


def project(features, qkv_weight, head_count):
    row_count, col_count, model_width = features.shape
    flat_rows = features.reshape(row_count * col_count, model_width)
    projected = lax.dot_general(qkv_weight, flat_rows, (((0,), (1,)), ((), ())), preferred_element_type=jnp.float32)
    return projected.astype(jnp.bfloat16).reshape(3, head_count, model_width // head_count, row_count, col_count)


def channels_first(grad_output, head_count):
    row_count, col_count, model_width = grad_output.shape
    return jnp.transpose(grad_output, (2, 0, 1)).reshape(head_count, model_width // head_count, row_count, col_count)


def query_side(queries, grad_cf, key_pad, value_pad, first_row, total_rows):
    head_count, head_size, row_count, col_count = queries.shape
    rim_rows = DILATION * (WINDOW // 2)
    score_scale = head_size ** -0.5
    score_list = []
    dot_list = []
    mask_list = []
    for a, b in window_pairs():
        key_slice = key_pad[:, :, DILATION * a:DILATION * a + row_count, DILATION * b:DILATION * b + col_count]
        value_slice = value_pad[:, :, DILATION * a:DILATION * a + row_count, DILATION * b:DILATION * b + col_count]
        score_list.append(score_scale * jnp.sum(queries.astype(jnp.float32) * key_slice.astype(jnp.float32), axis=1))
        dot_list.append(jnp.sum(grad_cf.astype(jnp.float32) * value_slice.astype(jnp.float32), axis=1))
        mask_list.append(inside(first_row, row_count, col_count, total_rows, DILATION * a - rim_rows, DILATION * b - rim_rows))
    scores = jnp.stack(score_list)
    value_dots = jnp.stack(dot_list)
    in_window = jnp.stack(mask_list)[:, None]
    masked = jnp.where(in_window, scores, -1e30)
    peak = jnp.max(masked, axis=0)
    expo = jnp.where(in_window, jnp.exp(masked - peak), 0.0)
    normaliser = jnp.sum(expo, axis=0)
    attend = expo / normaliser
    log_total = peak + jnp.log(normaliser)
    row_delta = jnp.sum(attend * value_dots, axis=0)
    dscore = attend * (value_dots - row_delta)
    grad_query = jnp.zeros(queries.shape, jnp.float32)
    for index, (a, b) in enumerate(window_pairs()):
        key_slice = key_pad[:, :, DILATION * a:DILATION * a + row_count, DILATION * b:DILATION * b + col_count]
        grad_query = grad_query + score_scale * dscore[index][:, None] * key_slice.astype(jnp.float32)
    return grad_query, log_total, row_delta, attend, dscore


def key_side(keys_own, values_own, query_pad, grad_pad, total_pad, delta_pad, first_row, total_rows):
    head_count, head_size, row_count, col_count = keys_own.shape
    rim_rows = DILATION * (WINDOW // 2)
    score_scale = head_size ** -0.5
    grad_key = jnp.zeros(keys_own.shape, jnp.float32)
    grad_value = jnp.zeros(keys_own.shape, jnp.float32)
    for a, b in window_pairs():
        row_from = DILATION * (WINDOW - 1 - a)
        col_from = DILATION * (WINDOW - 1 - b)
        query_slice = query_pad[:, :, row_from:row_from + row_count, col_from:col_from + col_count].astype(jnp.float32)
        grad_slice = grad_pad[:, :, row_from:row_from + row_count, col_from:col_from + col_count].astype(jnp.float32)
        total_slice = total_pad[:, row_from:row_from + row_count, col_from:col_from + col_count]
        delta_slice = delta_pad[:, row_from:row_from + row_count, col_from:col_from + col_count]
        in_window = inside(first_row, row_count, col_count, total_rows, rim_rows - DILATION * a, rim_rows - DILATION * b)[None]
        scores = score_scale * jnp.sum(query_slice * keys_own.astype(jnp.float32), axis=1)
        weight_now = jnp.where(in_window, jnp.exp(jnp.where(in_window, scores - total_slice, 0.0)), 0.0)
        value_dots = jnp.sum(grad_slice * values_own.astype(jnp.float32), axis=1)
        dscore = weight_now * (value_dots - delta_slice)
        grad_key = grad_key + score_scale * dscore[:, None] * query_slice
        grad_value = grad_value + weight_now[:, None] * grad_slice
    return grad_key, grad_value


def reference(features, qkv_weight, grad_output):
    height, col_count, model_width = features.shape
    head_count = HEADS
    rim_rows = DILATION * (WINDOW // 2)
    block_rows = ROWS_DEV * math.gcd(N_ROW, max(1, 64 // ROWS_DEV))
    block_count = height // block_rows
    zero = jnp.zeros((), jnp.int32)
    padded_features = jnp.pad(features, ((rim_rows, rim_rows), (0, 0), (0, 0)))
    padded_grad = jnp.pad(grad_output, ((rim_rows, rim_rows), (0, 0), (0, 0)))
    col_pad = ((0, 0), (0, 0), (0, 0), (rim_rows, rim_rows))

    def local(first_row):
        feature_block = lax.dynamic_slice_in_dim(padded_features, first_row, block_rows + 2 * rim_rows, 0)
        grad_block = lax.dynamic_slice_in_dim(padded_grad, first_row, block_rows + 2 * rim_rows, 0)
        return project(feature_block, qkv_weight, head_count), channels_first(grad_block, head_count)

    def pass_stats(block, state_pair):
        total_all, delta_all = state_pair
        first_row = (block * block_rows).astype(jnp.int32)
        qkv_block, grad_cf = local(first_row)
        queries = qkv_block[0][:, :, rim_rows:rim_rows + block_rows]
        grad_own = grad_cf[:, :, rim_rows:rim_rows + block_rows]
        key_pad = jnp.pad(qkv_block[1], col_pad)
        value_pad = jnp.pad(qkv_block[2], col_pad)
        grad_query, log_total, row_delta, attend, dscore = query_side(queries, grad_own, key_pad, value_pad, first_row, height)
        total_all = lax.dynamic_update_slice(total_all, log_total, (zero, first_row, zero))
        delta_all = lax.dynamic_update_slice(delta_all, row_delta, (zero, first_row, zero))
        return total_all, delta_all

    stat_shape = (head_count, height, col_count)
    total_all, delta_all = lax.fori_loop(0, block_count, pass_stats, (jnp.zeros(stat_shape, jnp.float32), jnp.zeros(stat_shape, jnp.float32)))
    stat_pad = ((0, 0), (rim_rows, rim_rows), (rim_rows, rim_rows))
    total_pad_all = jnp.pad(total_all, stat_pad)
    delta_pad_all = jnp.pad(delta_all, stat_pad)

    def pass_grads(block, state_pair):
        grad_all, weight_sum = state_pair
        first_row = (block * block_rows).astype(jnp.int32)
        qkv_block, grad_cf = local(first_row)
        queries = qkv_block[0][:, :, rim_rows:rim_rows + block_rows]
        keys_own = qkv_block[1][:, :, rim_rows:rim_rows + block_rows]
        values_own = qkv_block[2][:, :, rim_rows:rim_rows + block_rows]
        grad_own = grad_cf[:, :, rim_rows:rim_rows + block_rows]
        key_pad = jnp.pad(qkv_block[1], col_pad)
        value_pad = jnp.pad(qkv_block[2], col_pad)
        grad_query, log_total, row_delta, attend, dscore = query_side(queries, grad_own, key_pad, value_pad, first_row, height)
        query_pad = jnp.pad(qkv_block[0], col_pad)
        grad_pad = jnp.pad(grad_cf, col_pad)
        window_size = (head_count, block_rows + 2 * rim_rows, col_count + 2 * rim_rows)
        total_slice = lax.dynamic_slice(total_pad_all, (zero, first_row, zero), window_size)
        delta_slice = lax.dynamic_slice(delta_pad_all, (zero, first_row, zero), window_size)
        grad_key, grad_value = key_side(keys_own, values_own, query_pad, grad_pad, total_slice, delta_slice, first_row, height)
        grad_qkv = jnp.stack([grad_query, grad_key, grad_value]).astype(jnp.bfloat16)
        flat_grad = grad_qkv.reshape(3 * model_width, block_rows * col_count)
        grad_block = lax.dot_general(flat_grad, qkv_weight, (((0,), (1,)), ((), ())), preferred_element_type=jnp.float32)
        grad_block = grad_block.astype(jnp.bfloat16).reshape(block_rows, col_count, model_width)
        grad_all = lax.dynamic_update_slice(grad_all, grad_block, (first_row, zero, zero))
        feature_rows = lax.dynamic_slice_in_dim(features, first_row, block_rows, 0).reshape(block_rows * col_count, model_width)
        weight_sum = weight_sum + lax.dot_general(feature_rows, flat_grad, (((0,), (1,)), ((), ())), preferred_element_type=jnp.float32)
        return grad_all, weight_sum

    grad_all, weight_sum = lax.fori_loop(0, block_count, pass_grads, (jnp.zeros(features.shape, jnp.bfloat16), jnp.zeros((model_width, 3 * model_width), jnp.float32)))
    grad_weight = weight_sum * ((height * col_count) ** -0.5)
    return grad_all, grad_weight
```

```python
import functools
import jax
import jax.numpy as jnp
import numpy as np
from jax import lax
from jax.experimental import pallas as pl
from jax.experimental.pallas import tpu as pltpu
from jax.sharding import PartitionSpec as P

HEADS = 12
WINDOW = 7
DILATION = 2
HALO = 6
GROUPS = 3
BF = jnp.bfloat16
F32 = jnp.float32


def dot(a, b, ca=1, cb=0):
    return lax.dot_general(a, b, (((ca,), (cb,)), ((), ())), preferred_element_type=F32)


def column_maps():
    place = np.zeros((160, 128), np.float32)
    split = np.zeros((128, 128), np.float32)
    for col in range(128):
        place[80 * (col % 2) + col // 2 + 3, col] = 1
        split[64 * (col % 2) + col // 2, col] = 1
    return jnp.asarray(place, BF), jnp.asarray(split, BF)


def grads_kernel(edge_ref, x_ref, do_ref, w_ref, place_ref, split_ref,
                 dq_ref, acc_ref, dw_ref,
                 xk, xq, kv, q, do, bias, wkv):
    c = 32 ** -0.5 * 1.4426950408889634
    scale = 32 ** -0.5
    for g in range(GROUPS):
        wkv[:, 256 * g:256 * g + 128] = w_ref[:, 384 + 128 * g:384 + 128 * g + 128]
        wkv[:, 256 * g + 128:256 * g + 256] = w_ref[:, 768 + 128 * g:768 + 128 * g + 128]
    key = lax.broadcasted_iota(jnp.int32, (160, 128), 0)
    lane = lax.broadcasted_iota(jnp.int32, (160, 128), 1)
    krow, kcol = key // 16, key % 16
    qrow, qcol = (lane % 32) // 8, lane % 8
    drow, dcol = krow - qrow, kcol - qcol
    ok = (drow >= 0) & (drow <= 6) & (dcol >= 0) & (dcol <= 6)
    ok = ok & (krow >= edge_ref[0]) & (krow < edge_ref[1])
    for which, extra in enumerate((kcol >= 3, kcol >= 0, kcol < 11)):
        bias[which] = jnp.where(ok & extra, 0.0, -1e30).astype(F32)

    def project_row(row, carry):
        k, rp = row // 2, row % 2
        placed = dot(place_ref[...], x_ref[row]).astype(BF)
        xk[rp, 0, k] = placed[:80]
        xk[rp, 1, k] = placed[80:]
        both = dot(placed, wkv[...])
        for cp in range(2):
            for p in range(8):
                block = both[80 * cp + 8 * p:80 * cp + 8 * p + 16].astype(BF)
                for g in range(GROUPS):
                    kv[g, rp, cp, p, k] = block[:, 256 * g:256 * g + 256]
        return carry

    lax.fori_loop(0, 20, project_row, 0)
    for rp in range(2):
        for pair in range(2):
            row = 4 * pair + rp
            xs = [dot(split_ref[...], x_ref[6 + row + d]) for d in (0, 2)]
            ds = [dot(split_ref[...], do_ref[row + d]) for d in (0, 2)]
            for cp in range(2):
                for p in range(8):
                    at = slice(64 * cp + 8 * p, 64 * cp + 8 * p + 8)
                    xq[rp, cp, p, 16 * pair:16 * pair + 16] = jnp.concatenate([xs[0][at], xs[1][at]], axis=0).astype(BF)
                    dd = jnp.concatenate([ds[0][at], ds[1][at]], axis=0).astype(BF)
                    for g in range(GROUPS):
                        do[g, rp, cp, p, 16 * pair:16 * pair + 16] = dd[:, 128 * g:128 * g + 128]
        for cp in range(2):
            qs = dot(xq[rp, cp].reshape(256, 384), w_ref[:, :384]).astype(BF)
            for g in range(GROUPS):
                q[g, rp, cp] = qs[:, 128 * g:128 * g + 128].reshape(8, 32, 128)

    head_lane = lax.broadcasted_iota(jnp.int32, (32, 128), 1) // 32
    pick_b = [(head_lane == h).astype(F32).astype(BF) for h in range(4)]
    pick = [head_lane == h for h in range(4)]
    zero = jnp.zeros((128, 128), BF)

    def attend(step, carry):
        g, rp, cp = step // 4, (step // 2) % 2, step % 2
        tail = None
        for p in range(8):
            kvb = kv[g, rp, cp, p].reshape(160, 256)
            qp, dop = q[g, rp, cp, p], do[g, rp, cp, p]
            qbd = jnp.concatenate([qp * pick_b[h] for h in range(4)], axis=0)
            dobd = jnp.concatenate([dop * pick_b[h] for h in range(4)], axis=0)
            rhs = jnp.concatenate([jnp.concatenate([qbd, zero], axis=1), jnp.concatenate([zero, dobd], axis=1)], axis=0)
            s2 = dot(kvb, rhs, 1, 1)
            s = s2[:, :128] + bias[0 if p == 0 else (2 if p == 7 else 1)]
            dp = s2[:, 128:]
            m = jnp.max(s, axis=0, keepdims=True)
            e = jnp.exp2((s - m) * c)
            inv = 1.0 / jnp.sum(e, axis=0, keepdims=True)
            delta = jnp.sum(e * dp, axis=0, keepdims=True) * inv
            att = e * inv
            ds = att * (dp - delta)
            pd = jnp.concatenate([ds.astype(BF), att.astype(BF)], axis=1)
            dkv = dot(pd, rhs).reshape(10, 16, 256)
            head = dkv[:, :8]
            if tail is not None:
                head = head + tail
            acc_ref[g, rp, cp, :, 8 * p:8 * p + 8, :] = head
            tail = dkv[:, 8:]
            full = dot(pd[:, :128], kvb[:, :128], 0, 0)
            dq = jnp.where(pick[3], full[96:], 0.0)
            for h in range(3):
                dq = jnp.where(pick[h], full[32 * h:32 * h + 32], dq)
            dq_ref[g, rp, cp, p] = dq * scale
        acc_ref[g, rp, cp, :, 64:72, :] = tail
        acc_ref[g, rp, cp, :, 72:80, :] = jnp.zeros((10, 8, 256), F32)
        return carry

    lax.fori_loop(0, 12, attend, 0)

    dw = jnp.zeros((384, 768), F32)
    dwq = jnp.zeros((384, 384), F32)
    for rp in range(2):
        for cp in range(2):
            xs = xk[rp, cp].reshape(800, 384)
            parts = []
            for g in range(GROUPS):
                a = acc_ref[g, rp, cp].reshape(800, 256)
                parts.append((a[:, :128] * scale).astype(BF))
                parts.append(a[:, 128:].astype(BF))
            dw = dw + dot(xs, jnp.concatenate(parts, axis=1), 0, 0)
            dqs = jnp.concatenate([dq_ref[g, rp, cp].reshape(256, 128).astype(BF) for g in range(GROUPS)], axis=1)
            dwq = dwq + dot(xq[rp, cp].reshape(256, 384), dqs, 0, 0)
    dw_ref[:, :384] = dwq.astype(dw_ref.dtype)
    for g in range(GROUPS):
        dw_ref[:, 384 + 128 * g:512 + 128 * g] = dw[:, 256 * g:256 * g + 128].astype(dw_ref.dtype)
        dw_ref[:, 768 + 128 * g:896 + 128 * g] = dw[:, 256 * g + 128:256 * g + 256].astype(dw_ref.dtype)


def final_kernel(dq_ref, own_ref, above_ref, below_ref, w_ref, unplace_ref, unsplit_ref, out_ref):
    scale = 32 ** -0.5
    for rp in range(2):
        for kq in range(4):
            row = 2 * kq + rp
            dqs = jnp.concatenate(
                [jnp.concatenate([dq_ref[g, rp, cp, p, 8 * kq:8 * kq + 8] for g in range(GROUPS)], axis=1)
                 for cp in range(2) for p in range(8)], axis=0).astype(BF)
            ks, vs = [], []
            for g in range(GROUPS):
                both = []
                for cp in range(2):
                    t = own_ref[g, rp, cp, 3 + kq]
                    if kq < 3:
                        t = t + above_ref[g, rp, cp, kq].astype(F32)
                    if kq > 0:
                        t = t + below_ref[g, rp, cp, kq - 1].astype(F32)
                    both.append(t)
                both = jnp.concatenate(both, axis=0)
                ks.append((both[:, :128] * scale).astype(BF))
                vs.append(both[:, 128:].astype(BF))
            kvs = jnp.concatenate(ks + vs, axis=1)
            nq = dot(unsplit_ref[...], dqs).astype(BF)
            nkv = dot(unplace_ref[...], kvs).astype(BF)
            full = jnp.concatenate([nq, nkv], axis=1)
            out_ref[row] = dot(full, w_ref[...], 1, 1).astype(out_ref.dtype)


def halving_sum(x, axis):
    count = lax.axis_size(axis)
    index = lax.axis_index(axis)
    bits = count.bit_length() - 1
    x = x.reshape((2,) * bits + (x.shape[0] // count,) + x.shape[1:])
    for bit in range(bits):
        dim = bits - 1 - bit
        mine = (index >> bit) & 1
        keep = lax.dynamic_index_in_dim(x, mine, dim, keepdims=False)
        send = lax.dynamic_index_in_dim(x, 1 - mine, dim, keepdims=False).astype(BF)
        got = lax.ppermute(send, axis, [(i, i ^ (1 << bit)) for i in range(count)])
        x = keep.astype(F32) + got.astype(F32)
    return x


def shards(features, qkv_weight, grad_output):
    row_count, col_count, width = features.shape
    count = lax.axis_size("row")
    index = lax.axis_index("row")
    up = [(i, i + 1) for i in range(count - 1)]
    down = [(i + 1, i) for i in range(count - 1)]
    before = lax.ppermute(features[row_count - HALO:], "row", up)
    after = lax.ppermute(features[:HALO], "row", down)
    x20 = jnp.concatenate([before, features, after], axis=0)
    edge = jnp.stack([jnp.where(index == 0, 3, 0), jnp.where(index == count - 1, 7, 10)]).astype(jnp.int32)
    place, split = column_maps()
    vm = pl.BlockSpec(memory_space=pltpu.VMEM)
    dq, acc, dw = pl.pallas_call(
        grads_kernel,
        out_shape=(
            jax.ShapeDtypeStruct((GROUPS, 2, 2, 8, 32, 128), F32),
            jax.ShapeDtypeStruct((GROUPS, 2, 2, 10, 80, 256), F32),
            jax.ShapeDtypeStruct((384, 1152), F32),
        ),
        in_specs=[pl.BlockSpec(memory_space=pltpu.SMEM)] + [vm] * 5,
        out_specs=(vm, vm, vm),
        scratch_shapes=[
            pltpu.VMEM((2, 2, 10, 80, 384), BF),
            pltpu.VMEM((2, 2, 8, 32, 384), BF),
            pltpu.VMEM((GROUPS, 2, 2, 8, 10, 16, 256), BF),
            pltpu.VMEM((GROUPS, 2, 2, 8, 32, 128), BF),
            pltpu.VMEM((GROUPS, 2, 2, 8, 32, 128), BF),
            pltpu.VMEM((3, 160, 128), F32),
            pltpu.VMEM((384, 768), BF),
        ],
        compiler_params=pltpu.CompilerParams(vmem_limit_bytes=56 << 20),
        name="grads",
    )(edge, x20, grad_output, qkv_weight, place, split)
    from_above = lax.ppermute(acc[:, :, :, 7:].astype(BF), "row", up)
    from_below = lax.ppermute(acc[:, :, :, :3].astype(BF), "row", down)
    grad_features = pl.pallas_call(
        final_kernel,
        out_shape=jax.ShapeDtypeStruct(features.shape, BF),
        in_specs=[vm] * 7,
        out_specs=vm,
        compiler_params=pltpu.CompilerParams(vmem_limit_bytes=56 << 20),
        name="final",
    )(dq, acc, from_above, from_below, qkv_weight, place.T, split.T)
    summed = halving_sum(dw, "row")
    return grad_features, summed * (row_count * count * col_count) ** -0.5


def solution(mesh):
    placed = (P(("group", "row"), None, None), P(), P(("group", "row"), None, None))
    return jax.shard_map(
        shards,
        mesh=mesh,
        in_specs=placed,
        out_specs=(P(("group", "row"), None, None), P(("group", "row"), None)),
        check_vma=False,
    )
```

```python
import jax
import jax.numpy as jnp
import numpy as np
from jax import lax
from jax.experimental import pallas as pl
from jax.experimental.pallas import tpu as pltpu
from jax.sharding import PartitionSpec as P

HEADS = 12
WINDOW = 7
DILATION = 2
HALO = 6
GROUPS = 3
SLOTS = 4
BF = jnp.bfloat16
F32 = jnp.float32
SCALE = 32 ** -0.5
C = SCALE * 1.4426950408889634
VMEM_BYTES = 40 << 20


def dot(a, b, ca=1, cb=0):
    return lax.dot_general(a, b, (((ca,), (cb,)), ((), ())), preferred_element_type=F32)


def column_maps():
    place = np.zeros((160, 128), np.float32)
    split = np.zeros((128, 128), np.float32)
    for col in range(128):
        place[80 * (col % 2) + col // 2 + 3, col] = 1
        split[64 * (col % 2) + col // 2, col] = 1
    return jnp.asarray(place, BF), jnp.asarray(split, BF)


def gather_kv_weight(w_ref, wkv):
    for g in range(GROUPS):
        wkv[:, 256 * g:256 * g + 128] = w_ref[:, 384 + 128 * g:384 + 128 * g + 128]
        wkv[:, 256 * g + 128:256 * g + 256] = w_ref[:, 768 + 128 * g:768 + 128 * g + 128]


def project_keys(x, place_ref, wkv, xk, kv, k):
    placed = dot(place_ref[...], x).astype(BF)
    xk[0, k] = placed[:80]
    xk[1, k] = placed[80:]
    both = dot(placed, wkv[...])
    for cp in range(2):
        for p in range(8):
            block = both[80 * cp + 8 * p:80 * cp + 8 * p + 16].astype(BF)
            for g in range(GROUPS):
                kv[g, cp, p, k] = block[:, 256 * g:256 * g + 256]


def to_patches(pair_rows, split_ref, store):
    parts = [None if row is None else dot(split_ref[...], row) for row in pair_rows]
    for cp in range(2):
        for p in range(8):
            at = slice(64 * cp + 8 * p, 64 * cp + 8 * p + 8)
            known = [part for part in parts if part is not None][0][at]
            halves = [jnp.zeros_like(known) if part is None else part[at] for part in parts]
            store(cp, p, jnp.concatenate(halves, axis=0).astype(BF))


def pack_kernel(edge_ref, x_ref, g_ref, x0_ref, x1_ref, fg_ref, near_ref, xs, gs, sem):
    odd = edge_ref[2]
    mine, other = pl.ds(odd, 3), pl.ds(1 - odd, 3)
    loads = [pltpu.make_async_copy(x_ref, xs, sem.at[0]), pltpu.make_async_copy(g_ref, gs, sem.at[1])]
    for copy in loads:
        copy.start()
    loads[0].wait()
    copies = [
        pltpu.make_async_copy(xs.at[mine, 0], x0_ref, sem.at[2]),
        pltpu.make_async_copy(xs.at[other], near_ref.at[0], sem.at[3]),
        pltpu.make_async_copy(xs.at[mine, 1], x1_ref, sem.at[4]),
        pltpu.make_async_copy(gs.at[other], near_ref.at[1], sem.at[5]),
        pltpu.make_async_copy(gs.at[mine], fg_ref, sem.at[6]),
    ]
    for copy in copies[:3]:
        copy.start()
    loads[1].wait()
    for copy in copies[3:]:
        copy.start()
    for copy in copies:
        copy.wait()


def own_kernel(x_ref, do_ref, w_ref, place_ref, split_ref, q_ref, g_ref, xq_ref, kv_ref, xk_ref, wkv):
    gather_kv_weight(w_ref, wkv)
    for rp in range(2):
        for k in range(4):
            project_keys(x_ref[k, rp], place_ref, wkv, xk_ref.at[rp], kv_ref.at[rp], k)
        for pair in range(2):
            at = slice(16 * pair, 16 * pair + 16)

            def store_x(cp, p, block, at=at, rp=rp):
                xq_ref[rp, cp, p, at] = block

            def store_g(cp, p, block, at=at, rp=rp):
                for g in range(GROUPS):
                    g_ref[rp, g, cp, p, at] = block[:, 128 * g:128 * g + 128]

            to_patches([x_ref[2 * pair + d, rp] for d in range(2)], split_ref, store_x)
            to_patches([do_ref[2 * pair + d, rp] for d in range(2)], split_ref, store_g)
        for cp in range(2):
            qs = dot(xq_ref[rp, cp].reshape(256, 384), w_ref[:, :384]).astype(BF)
            for g in range(GROUPS):
                q_ref[rp, g, cp] = qs[:, 128 * g:128 * g + 128].reshape(8, 32, 128)


def window_bias(bias, key_rows, row_ok):
    shape = (16 * key_rows, 128)
    key = lax.broadcasted_iota(jnp.int32, shape, 0)
    lane = lax.broadcasted_iota(jnp.int32, shape, 1)
    krow, kcol = key // 16, key % 16
    qrow, dcol = (lane % 32) // 8, key % 16 - lane % 8
    ok = row_ok(krow, qrow) & (dcol >= 0) & (dcol <= 6)
    for which, extra in enumerate((kcol >= 3, kcol >= 0, kcol < 11)):
        bias[which] = jnp.where(ok & extra, 0.0, -1e30).astype(F32)


def head_masks():
    head_lane = lax.broadcasted_iota(jnp.int32, (32, 128), 1) // 32
    return [head_lane == h for h in range(4)], [(head_lane == h).astype(F32).astype(BF) for h in range(4)]


def pack_heads(rhs, slot, qp, gp, pick_b):
    for h in range(4):
        rhs[slot, 32 * h:32 * h + 32, :128] = qp * pick_b[h]
        rhs[slot, 128 + 32 * h:160 + 32 * h, 128:] = gp * pick_b[h]


def clear_off_diagonal(rhs):
    for slot in range(rhs.shape[0]):
        rhs[slot, :128, 128:] = jnp.zeros((128, 128), BF)
        rhs[slot, 128:, :128] = jnp.zeros((128, 128), BF)


def edge_kind(p):
    return 0 if p == 0 else (2 if p == 7 else 1)


def attend_kernel(rp, edge_ref, near_ref, far_ref, q, do, xq, kv, xk, w_ref, place_ref, *refs):
    if rp == 0:
        dw_in = None
    else:
        dw_in, *refs = refs
    dq_ref, own_ref, stat_ref, dw_ref, xh, kvh, acc, bias, wkv, sc, pd, rhs, tail = refs
    odd = edge_ref[2]
    gather_kv_weight(w_ref, wkv)
    window_bias(bias, 10, lambda krow, qrow: (krow >= qrow) & (krow <= qrow + 6) & (krow >= edge_ref[0]) & (krow < edge_ref[1]))

    def project_pair(k, carry):
        project_keys(near_ref[0, k, rp], place_ref, wkv, xh, kvh, k + 3 - 3 * odd)
        project_keys(far_ref[k], place_ref, wkv, xh, kvh, k + 3 * odd)
        return carry

    lax.fori_loop(0, 3, project_pair, 0)
    pick, pick_b = head_masks()
    clear_off_diagonal(rhs)

    def attend(step, carry):
        g, cp = step // 2, step % 2

        def keys(p):
            return jnp.concatenate([
                kvh[g, cp, p, :3].reshape(48, 256),
                kv[0, g, cp, p].reshape(64, 256),
                kvh[g, cp, p, 3:].reshape(48, 256)], axis=0)

        def score(p):
            slot = p % SLOTS
            pack_heads(rhs, slot, q[0, g, cp, p], do[0, g, cp, p], pick_b)
            sc[p % 2] = dot(keys(p), rhs[slot], 1, 1)

        def soften(p):
            slot = p % 2
            s = sc[slot, :, :128] + bias[edge_kind(p)]
            m = jnp.max(s, axis=0, keepdims=True)
            e = jnp.exp2((s - m) * C)
            dp = sc[slot, :, 128:]
            total = jnp.sum(e, axis=0, keepdims=True)
            inv = 1.0 / total
            delta = jnp.sum(e * dp, axis=0, keepdims=True) * inv
            att = e * inv
            pd[slot, :, :128] = (att * (dp - delta)).astype(BF)
            pd[slot, :, 128:] = att.astype(BF)
            stat_ref[0, g, cp, p:p + 1] = m * C + jnp.log2(total)
            stat_ref[1, g, cp, p:p + 1] = delta

        def add_to(at, value):
            acc[g, cp, :3, at, :] = value[:3]
            own_ref[g, cp, :, at, :] = value[3:7]
            acc[g, cp, 3:, at, :] = value[7:]

        def spread(p):
            slot = p % 2
            dkv = dot(pd[slot], rhs[p % SLOTS]).reshape(10, 16, 256)
            head = dkv[:, :8]
            if p > 0:
                head = head + tail[(p + 1) % 2]
            add_to(slice(8 * p, 8 * p + 8), head)
            if p < 7:
                tail[slot] = dkv[:, 8:]
            else:
                add_to(slice(64, 72), dkv[:, 8:])
            full = dot(pd[slot, :, :128], keys(p)[:, :128], 0, 0)
            dq = jnp.where(pick[3], full[96:], 0.0)
            for h in range(3):
                dq = jnp.where(pick[h], full[32 * h:32 * h + 32], dq)
            dq_ref[g, cp, p] = (dq * SCALE).astype(BF)

        for t in range(8 + 2):
            if t < 8:
                score(t)
            if 0 <= t - 1 < 8:
                soften(t - 1)
            if 0 <= t - 2 < 8:
                spread(t - 2)
        add_to(slice(72, 80), jnp.zeros((10, 8, 256), F32))
        return carry

    lax.fori_loop(0, 6, attend, 0)

    dw = jnp.zeros((384, 768), F32)
    dwq = jnp.zeros((384, 384), F32)
    for cp in range(2):
        for xs, ref, n in ((xh[cp], acc, 480), (xk[0, cp], own_ref, 320)):
            parts = []
            for g in range(GROUPS):
                a = ref[g, cp].reshape(n, 256)
                parts.append((a[:, :128] * SCALE).astype(BF))
                parts.append(a[:, 128:].astype(BF))
            dw = dw + dot(xs.reshape(n, 384), jnp.concatenate(parts, axis=1), 0, 0)
        dqs = jnp.concatenate([dq_ref[g, cp].reshape(256, 128) for g in range(GROUPS)], axis=1)
        dwq = dwq + dot(xq[0, cp].reshape(256, 384), dqs, 0, 0)

    def put(at, value):
        dw_ref[:, at:at + value.shape[1]] = value if dw_in is None else value + dw_in[:, at:at + value.shape[1]]

    put(0, dwq)
    for g in range(GROUPS):
        put(384 + 128 * g, dw[:, 256 * g:256 * g + 128])
        put(768 + 128 * g, dw[:, 256 * g + 128:256 * g + 256])


def cross_kernel(rp, edge_ref, near_ref, far_ref, far_g_ref, near_stat, far_stat, kv, own_ref, w_ref, split_ref,
                 dkvs, xq, q, do, bias_a, bias_b, sc, pd, rhs, acc, tail, stats):
    odd = edge_ref[2]
    stats[1 - odd] = near_stat[...]
    stats[odd] = far_stat[...]
    window_bias(bias_a, 3, lambda krow, qrow: krow <= qrow - 1)
    window_bias(bias_b, 3, lambda krow, qrow: krow >= qrow)
    pick, pick_b = head_masks()
    clear_off_diagonal(rhs)
    sides = ((0, bias_a), (1, bias_b))

    def side_patches(side, x_row, d_row):
        lines = [None, 0, 1, 2] if side == 0 else [0, 1, 2, None]
        for pair in range(2):
            rows = lines[2 * pair:2 * pair + 2]
            at = slice(16 * pair, 16 * pair + 16)

            def store_x(cp, p, block, at=at):
                xq[cp, p, at] = block

            def store_g(cp, p, block, at=at):
                for g in range(GROUPS):
                    do[side, g, cp, p, at] = block[:, 128 * g:128 * g + 128]

            to_patches([None if r is None else x_row(r) for r in rows], split_ref, store_x)
            to_patches([None if r is None else d_row(r) for r in rows], split_ref, store_g)
        for cp in range(2):
            qs = dot(xq[cp].reshape(256, 384), w_ref[:, :384]).astype(BF)
            for g in range(GROUPS):
                q[side, g, cp] = qs[:, 128 * g:128 * g + 128].reshape(8, 32, 128)

    for parity in range(2):
        @pl.when(odd == parity)
        def _(parity=parity):
            side_patches(1 - parity, lambda r: near_ref[0, r, rp], lambda r: near_ref[1, r, rp])
            side_patches(parity, lambda r: far_ref[r], lambda r: far_g_ref[r, rp])

    def attend(step, carry):
        g, cp = step // 2, step % 2

        def score(p):
            for side, bias in sides:
                slot = 2 * (p % SLOTS) + side
                pack_heads(rhs, slot, q[side, g, cp, p], do[side, g, cp, p], pick_b)
                sc[2 * (p % 2) + side] = dot(kv[0, g, cp, p, side:side + 3].reshape(48, 256), rhs[slot], 1, 1)

        def soften(p):
            for side, bias in sides:
                slot = 2 * (p % 2) + side
                s = (sc[slot, :, :128] + bias[edge_kind(p)]) * C
                att = jnp.exp2(s - stats[side, 0, g, cp, p:p + 1])
                ds = att * (sc[slot, :, 128:] - stats[side, 1, g, cp, p:p + 1])
                pd[slot, :, :128] = ds.astype(BF)
                pd[slot, :, 128:] = att.astype(BF)

        def spread(p):
            up, down = (dot(pd[2 * (p % 2) + side], rhs[2 * (p % SLOTS) + side]).reshape(3, 16, 256) for side in range(2))
            dkv = jnp.concatenate([up[:1], up[1:] + down[:2], down[2:]], axis=0)
            head = dkv[:, :8] + own_ref[g, cp, :, 8 * p:8 * p + 8, :]
            if p > 0:
                head = head + tail[(p + 1) % 2]
            acc[:, 8 * p:8 * p + 8, :] = head
            if p < 7:
                tail[p % 2] = dkv[:, 8:]
            else:
                acc[:, 64:72, :] = dkv[:, 8:] + own_ref[g, cp, :, 64:72, :]

        for t in range(8 + 2):
            if t < 8:
                score(t)
            if 0 <= t - 1 < 8:
                soften(t - 1)
            if 0 <= t - 2 < 8:
                spread(t - 2)
        acc[:, 72:80, :] = jnp.zeros((4, 8, 256), F32)
        dkvs[g, cp, :, :, :128] = (acc[:, :, :128] * SCALE).astype(BF)
        dkvs[g, cp, :, :, 128:] = acc[:, :, 128:].astype(BF)
        return carry

    lax.fori_loop(0, 6, attend, 0)


def final_kernel(dq0_ref, dq1_ref, dkv0_ref, dkv1_ref, w_ref, unplace_ref, unsplit_ref, out_ref):
    for rp, (dq_ref, dkvs) in enumerate(((dq0_ref, dkv0_ref), (dq1_ref, dkv1_ref))):
        for pair in range(2):
            quads = [jnp.concatenate([dq_ref[g, cp, p, 16 * pair:16 * pair + 16] for g in range(GROUPS)], axis=1).astype(F32)
                     for cp in range(2) for p in range(8)]
            for sub in range(2):
                kq = 2 * pair + sub
                dqs = jnp.concatenate([t[8 * sub:8 * sub + 8] for t in quads], axis=0).astype(BF)
                parts = [jnp.concatenate([dkvs[g, 0, kq], dkvs[g, 1, kq]], axis=0) for g in range(GROUPS)]
                both = jnp.concatenate([t[:, :128] for t in parts] + [t[:, 128:] for t in parts], axis=1)
                nq = dot(unsplit_ref[...], dqs).astype(BF)
                nkv = dot(unplace_ref[...], both).astype(BF)
                out_ref[2 * kq + rp] = dot(jnp.concatenate([nq, nkv], axis=1), w_ref[...], 1, 1).astype(BF)


def after(value, *others):
    return lax.optimization_barrier((value,) + others)[0]


def exchange(x, axis, dim, bit_count, low, behind):
    count = lax.axis_size(axis)
    span = 1 << bit_count
    mine = (lax.axis_index(axis) >> low) & (span - 1)
    total = lax.dynamic_index_in_dim(x, mine, dim, keepdims=False).astype(F32)
    sent = [lax.ppermute(lax.dynamic_index_in_dim(x, mine ^ turn, dim, keepdims=False).astype(BF), axis,
                         [(i, i ^ (turn << low)) for i in range(count)]) for turn in range(1, span)]
    for block in lax.optimization_barrier((behind, *sent))[1:]:
        total = total + block.astype(F32)
    return total


def block(shape, *at):
    at = at + (0,) * (len(shape) - len(at))
    return pl.BlockSpec(shape, lambda i: at)


def whole(x):
    return block(x.shape)


SMEM = pl.BlockSpec(memory_space=pltpu.SMEM)
ANY = pl.BlockSpec(memory_space=pl.ANY)


def call(kernel, name, us, outs, out_specs, scratch, args, in_specs, aliases={}):
    return pl.pallas_call(
        kernel,
        grid=(1,),
        out_shape=[jax.ShapeDtypeStruct(s, t) for s, t in outs],
        in_specs=in_specs,
        out_specs=out_specs,
        scratch_shapes=[pltpu.VMEM(s, t) for s, t in scratch],
        compiler_params=pltpu.CompilerParams(vmem_limit_bytes=VMEM_BYTES),
        cost_estimate=pl.CostEstimate(flops=int(us * 1e9), bytes_accessed=1 << 20, transcendentals=0),
        input_output_aliases=aliases,
        name=name,
    )(*args)


def pack_call(edge, x4, g4):
    rows = x4.shape[2:]
    return pl.pallas_call(
        pack_kernel,
        out_shape=[jax.ShapeDtypeStruct(s + rows, BF) for s in ((3,), (3,), (3, 2), (2, 3, 2))],
        in_specs=[SMEM, ANY, ANY],
        out_specs=[ANY] * 4,
        scratch_shapes=[pltpu.VMEM(x4.shape, BF), pltpu.VMEM(g4.shape, BF), pltpu.SemaphoreType.DMA((7,))],
        name="pack",
    )(edge, x4, g4)


def own_call(x4, g4, w, place, split):
    outs = [((2, 3, 2, 8, 32, 128), BF), ((2, 3, 2, 8, 32, 128), BF), ((2, 2, 8, 32, 384), BF),
            ((2, 3, 2, 8, 4, 16, 256), BF), ((2, 2, 4, 80, 384), BF)]
    args = (x4, g4, w, place, split)
    return call(own_kernel, "own", 4, outs, [block(s) for s, _ in outs], [((384, 768), BF)], args, [whole(a) for a in args])


def attend_call(rp, edge, near, far, q, do, xq, kv, xk, w, place, dw):
    def kernel(*refs):
        attend_kernel(rp, *refs)

    outs = [((3, 2, 8, 32, 128), BF), ((3, 2, 4, 80, 256), F32), ((2, 3, 2, 8, 128), F32), ((384, 1152), F32)]
    args = [edge, near, far, q, do, xq, kv, xk, w, place]
    specs = [SMEM, whole(near), whole(far)] + [block((1,) + a.shape[1:], rp) for a in (q, do, xq, kv, xk)] + [whole(w), whole(place)]
    if rp == 1:
        args.append(dw)
        specs.append(whole(dw))
    return call(kernel, "attend", 12, outs, [block(s) for s, _ in outs], [
        ((2, 6, 80, 384), BF), ((3, 2, 8, 6, 16, 256), BF), ((3, 2, 6, 80, 256), F32), ((3, 160, 128), F32),
        ((384, 768), BF), ((2, 160, 256), F32), ((2, 160, 256), BF), ((SLOTS, 256, 256), BF), ((2, 10, 8, 256), F32),
    ], args, specs)


def cross_call(rp, edge, near, far, far_g, stat_near, stat_far, kv, own, w, split):
    def kernel(*refs):
        cross_kernel(rp, *refs)

    args = [edge, near, far, far_g, stat_near, stat_far, kv, own, w, split]
    specs = [SMEM] + [whole(a) for a in args[1:6]] + [block((1,) + kv.shape[1:], rp)] + [whole(a) for a in args[7:]]
    return call(kernel, "cross", 9, [((3, 2, 4, 80, 256), BF)], [block((3, 2, 4, 80, 256))], [
        ((2, 8, 32, 384), BF), ((2, 3, 2, 8, 32, 128), BF), ((2, 3, 2, 8, 32, 128), BF),
        ((3, 48, 128), F32), ((3, 48, 128), F32), ((4, 48, 256), F32), ((4, 48, 256), BF),
        ((2 * SLOTS, 256, 256), BF), ((4, 80, 256), F32), ((2, 4, 8, 256), F32), ((2, 2, 3, 2, 8, 128), F32),
    ], args, specs)[0]


def final_call(shape, *args):
    return call(final_kernel, "final", 4, [(shape, BF)], [block(shape)], [], args, [whole(a) for a in args])[0]


def shards(features, qkv_weight, grad_output):
    row_count, col_count, width = features.shape
    count = lax.axis_size("row")
    index = lax.axis_index("row")
    odd = index & 1
    near = [(i, i ^ 1) for i in range(count)]
    far = [(i, i + 1) for i in range(1, count - 1, 2)] + [(i + 1, i) for i in range(1, count - 1, 2)]
    place, split = column_maps()
    edge = jnp.stack([jnp.where(index == 0, 3, 0), jnp.where(index == count - 1, 7, 10), odd]).astype(jnp.int32)
    x4, g4 = (a.reshape(row_count // 2, 2, col_count, width) for a in (features, grad_output))
    send_x0, send_x1, send_g, send_near = pack_call(edge, x4, g4)

    far_x0 = lax.ppermute(send_x0, "row", far)
    near_xg = lax.ppermute(send_near, "row", near)
    q, do, xq, kv, xk = own_call(x4, g4, qkv_weight, place, split)
    far_x1 = lax.ppermute(after(send_x1, far_x0, xk), "row", far)
    dq0, own0, stat0, dw0 = attend_call(0, edge, near_xg, far_x0, q, do, xq, kv, xk, qkv_weight, place, None)
    far_x1 = after(far_x1, dw0)
    far_g = lax.ppermute(after(send_g, far_x1), "row", far)
    stat0_near = lax.ppermute(stat0, "row", near)
    stat0_far = lax.ppermute(stat0, "row", far)
    dq1, own1, stat1, dw1 = attend_call(1, edge, near_xg, far_x1, q, do, xq, kv, xk, qkv_weight, place, dw0)
    far_g, stat0_near, stat0_far, _ = lax.optimization_barrier((far_g, stat0_near, stat0_far, dq1))
    stat1_near = lax.ppermute(stat1, "row", near)
    stat1_far = lax.ppermute(stat1, "row", far)
    bits = count.bit_length() - 1
    rows = width // count
    dkv0 = cross_call(0, edge, near_xg, far_x0, far_g, stat0_near, stat0_far, kv, own0, qkv_weight, split)
    stat1_near, stat1_far, _ = lax.optimization_barrier((stat1_near, stat1_far, dkv0))
    total = exchange(dw1.reshape(count // 2, 2, rows, 3 * width), "row", 1, 1, 0, dkv0)
    dkv1 = cross_call(1, edge, near_xg, far_x1, far_g, stat1_near, stat1_far, kv, own1, qkv_weight, split)
    total = exchange(total.reshape(count // 4, 2, rows, 3 * width), "row", 1, 1, 1, dkv1)
    grad_features = final_call(features.shape, dq0, dq1, dkv0, dkv1, qkv_weight, place.T, split.T)
    low = 2
    while low < bits:
        step = min(2, bits - low)
        total = exchange(total.reshape(count >> (low + step), 1 << step, rows, 3 * width), "row", 1, step, low, grad_features)
        low += step
    grad_weight = total.reshape(rows, 3 * width) * (row_count * count * col_count) ** -0.5
    return grad_features, grad_weight


def solution(mesh):
    placed = (P(("group", "row"), None, None), P(), P(("group", "row"), None, None))
    return jax.shard_map(
        shards,
        mesh=mesh,
        in_specs=placed,
        out_specs=(P(("group", "row"), None, None), P(("group", "row"), None)),
        check_vma=False,
    )
```

```python
import jax
import jax.numpy as jnp
import numpy as np
from jax import lax
from jax.experimental import pallas as pl
from jax.experimental.pallas import tpu as pltpu
from jax.sharding import PartitionSpec as P

HEADS = 12
WINDOW = 7
DILATION = 2
HALO = 6
GROUPS = 3
UNITS = 16
LAG = 3
SLOTS = 2 * LAG + 1
CROSS_UNITS = 16
BF = jnp.bfloat16
F32 = jnp.float32
SCALE = 32 ** -0.5
C = SCALE * 1.4426950408889634
VMEM_BYTES = 40 << 20


def dot(a, b, ca=1, cb=0):
    return lax.dot_general(a, b, (((ca,), (cb,)), ((), ())), preferred_element_type=F32)


def column_maps():
    place = np.zeros((160, 128), np.float32)
    split = np.zeros((128, 128), np.float32)
    for col in range(128):
        place[80 * (col % 2) + col // 2 + 3, col] = 1
        split[64 * (col % 2) + col // 2, col] = 1
    return jnp.asarray(place, BF), jnp.asarray(split, BF)


def gather_kv_weight(w_ref, wkv):
    for g in range(GROUPS):
        wkv[:, 256 * g:256 * g + 128] = w_ref[:, 384 + 128 * g:384 + 128 * g + 128]
        wkv[:, 256 * g + 128:256 * g + 256] = w_ref[:, 768 + 128 * g:768 + 128 * g + 128]


def project_keys(x, place_ref, wkv, xk, kv, k):
    placed = dot(place_ref[...], x).astype(BF)
    xk[0, k] = placed[:80]
    xk[1, k] = placed[80:]
    both = dot(placed, wkv[...])
    for cp in range(2):
        for p in range(8):
            block = both[80 * cp + 8 * p:80 * cp + 8 * p + 16].astype(BF)
            for g in range(GROUPS):
                kv[g, cp, p, k] = block[:, 256 * g:256 * g + 256]


def to_patches(pair_rows, split_ref, store):
    parts = [None if row is None else dot(split_ref[...], row) for row in pair_rows]
    for cp in range(2):
        for p in range(8):
            at = slice(64 * cp + 8 * p, 64 * cp + 8 * p + 8)
            known = [part for part in parts if part is not None][0][at]
            halves = [jnp.zeros_like(known) if part is None else part[at] for part in parts]
            store(cp, p, jnp.concatenate(halves, axis=0).astype(BF))


def pack_kernel(edge_ref, x_ref, g_ref, x0_ref, x1_ref, fg_ref, near_ref, xs, gs, sem):
    odd = edge_ref[2]
    mine, other = pl.ds(odd, 3), pl.ds(1 - odd, 3)
    loads = [pltpu.make_async_copy(x_ref, xs, sem.at[0]), pltpu.make_async_copy(g_ref, gs, sem.at[1])]
    for copy in loads:
        copy.start()
    loads[0].wait()
    copies = [
        pltpu.make_async_copy(xs.at[mine, 0], x0_ref, sem.at[2]),
        pltpu.make_async_copy(xs.at[other], near_ref.at[0], sem.at[3]),
        pltpu.make_async_copy(xs.at[mine, 1], x1_ref, sem.at[4]),
        pltpu.make_async_copy(gs.at[other], near_ref.at[1], sem.at[5]),
        pltpu.make_async_copy(gs.at[mine], fg_ref, sem.at[6]),
    ]
    for copy in copies[:3]:
        copy.start()
    loads[1].wait()
    for copy in copies[3:]:
        copy.start()
    for copy in copies:
        copy.wait()


def own_kernel(x_ref, do_ref, w_ref, place_ref, split_ref, q_ref, g_ref, xq_ref, kv_ref, xk_ref, wkv):
    gather_kv_weight(w_ref, wkv)
    for rp in range(2):
        for k in range(4):
            project_keys(x_ref[k, rp], place_ref, wkv, xk_ref.at[rp], kv_ref.at[rp], k)
        for pair in range(2):
            at = slice(16 * pair, 16 * pair + 16)

            def store_x(cp, p, block, at=at, rp=rp):
                xq_ref[rp, cp, p, at] = block

            def store_g(cp, p, block, at=at, rp=rp):
                for g in range(GROUPS):
                    g_ref[rp, g, cp, p, at] = block[:, 128 * g:128 * g + 128]

            to_patches([x_ref[2 * pair + d, rp] for d in range(2)], split_ref, store_x)
            to_patches([do_ref[2 * pair + d, rp] for d in range(2)], split_ref, store_g)
        for cp in range(2):
            qs = dot(xq_ref[rp, cp].reshape(256, 384), w_ref[:, :384]).astype(BF)
            for g in range(GROUPS):
                q_ref[rp, g, cp] = qs[:, 128 * g:128 * g + 128].reshape(8, 32, 128)


def window_bias(bias, key_rows, row_ok):
    shape = (16 * key_rows, 128)
    key = lax.broadcasted_iota(jnp.int32, shape, 0)
    lane = lax.broadcasted_iota(jnp.int32, shape, 1)
    krow, kcol = key // 16, key % 16
    qrow, dcol = (lane % 32) // 8, key % 16 - lane % 8
    ok = row_ok(krow, qrow) & (dcol >= 0) & (dcol <= 6)
    for which, extra in enumerate((kcol >= 3, kcol >= 0, kcol < 11)):
        bias[which] = jnp.where(ok & extra, 0.0, -1e30).astype(F32)


def head_masks():
    head_lane = lax.broadcasted_iota(jnp.int32, (32, 128), 1) // 32
    return [head_lane == h for h in range(4)], [(head_lane == h).astype(F32).astype(BF) for h in range(4)]


def pack_heads(rhs, slot, qp, gp, pick_b):
    for h in range(4):
        rhs[slot, 32 * h:32 * h + 32, :128] = qp * pick_b[h]
        rhs[slot, 128 + 32 * h:160 + 32 * h, 128:] = gp * pick_b[h]


def clear_off_diagonal(rhs):
    for slot in range(rhs.shape[0]):
        rhs[slot, :128, 128:] = jnp.zeros((128, 128), BF)
        rhs[slot, 128:, :128] = jnp.zeros((128, 128), BF)


def edge_kind(p):
    return 0 if p == 0 else (2 if p == 7 else 1)


def attend_kernel(rp, edge_ref, near_ref, far_ref, q, do, xq, kv, xk, w_ref, place_ref, *refs):
    if rp == 0:
        dw_in = None
    else:
        dw_in, *refs = refs
    dq_ref, own_ref, stat_ref, dw_ref, xh, kvh, acc, bias, wkv, sc, pd, rhs, tail = refs
    odd = edge_ref[2]
    gather_kv_weight(w_ref, wkv)
    window_bias(bias, 10, lambda krow, qrow: (krow >= qrow) & (krow <= qrow + 6) & (krow >= edge_ref[0]) & (krow < edge_ref[1]))

    def project_pair(k, carry):
        project_keys(near_ref[0, k, rp], place_ref, wkv, xh, kvh, k + 3 - 3 * odd)
        project_keys(far_ref[k], place_ref, wkv, xh, kvh, k + 3 * odd)
        return carry

    lax.fori_loop(0, 3, project_pair, 0)
    pick, pick_b = head_masks()
    clear_off_diagonal(rhs)

    def attend(step, carry):
        def place_of(u):
            index = step * (UNITS // 8) + u // 8
            return index // 2, (index % 2 if UNITS == 8 else u // 8), u % 8

        def keys(u):
            g, cp, p = place_of(u)
            return jnp.concatenate([
                kvh[g, cp, p, :3].reshape(48, 256),
                kv[0, g, cp, p].reshape(64, 256),
                kvh[g, cp, p, 3:].reshape(48, 256)], axis=0)

        def score(u):
            g, cp, p = place_of(u)
            pack_heads(rhs, u % SLOTS, q[0, g, cp, p], do[0, g, cp, p], pick_b)
            sc[u % (LAG + 1)] = dot(keys(u), rhs[u % SLOTS], 1, 1)

        def soften(u):
            g, cp, p = place_of(u)
            now, slot = u % (LAG + 1), u % (LAG + 1)
            s = sc[now, :, :128] + bias[edge_kind(p)]
            m = jnp.max(s, axis=0, keepdims=True)
            e = jnp.exp2((s - m) * C)
            dp = sc[now, :, 128:]
            total = jnp.sum(e, axis=0, keepdims=True)
            inv = 1.0 / total
            delta = jnp.sum(e * dp, axis=0, keepdims=True) * inv
            att = e * inv
            pd[slot, :, :128] = (att * (dp - delta)).astype(BF)
            pd[slot, :, 128:] = att.astype(BF)
            stat_ref[0, g, cp, p:p + 1] = m * C + jnp.log2(total)
            stat_ref[1, g, cp, p:p + 1] = delta

        def spread(u):
            g, cp, p = place_of(u)
            slot = u % (LAG + 1)

            def add_to(at, value):
                acc[g, cp, :3, at, :] = value[:3]
                own_ref[g, cp, :, at, :] = value[3:7]
                acc[g, cp, 3:, at, :] = value[7:]

            dkv = dot(pd[slot], rhs[u % SLOTS]).reshape(10, 16, 256)
            head = dkv[:, :8]
            if p > 0:
                head = head + tail[(p + 1) % 2]
            add_to(slice(8 * p, 8 * p + 8), head)
            if p < 7:
                tail[p % 2] = dkv[:, 8:]
            else:
                add_to(slice(64, 72), dkv[:, 8:])
                add_to(slice(72, 80), jnp.zeros((10, 8, 256), F32))
            full = dot(pd[slot, :, :128], keys(u)[:, :128], 0, 0)
            dq = jnp.where(pick[3], full[96:], 0.0)
            for h in range(3):
                dq = jnp.where(pick[h], full[32 * h:32 * h + 32], dq)
            dq_ref[g, cp, p] = (dq * SCALE).astype(BF)

        for t in range(UNITS + 2 * LAG):
            if t < UNITS:
                score(t)
            if 0 <= t - LAG < UNITS:
                soften(t - LAG)
            if 0 <= t - 2 * LAG < UNITS:
                spread(t - 2 * LAG)
        return carry

    lax.fori_loop(0, 48 // UNITS, attend, 0)

    dw = jnp.zeros((384, 768), F32)
    dwq = jnp.zeros((384, 384), F32)
    for cp in range(2):
        for xs, ref, n in ((xh[cp], acc, 480), (xk[0, cp], own_ref, 320)):
            parts = []
            for g in range(GROUPS):
                a = ref[g, cp].reshape(n, 256)
                parts.append((a[:, :128] * SCALE).astype(BF))
                parts.append(a[:, 128:].astype(BF))
            dw = dw + dot(xs.reshape(n, 384), jnp.concatenate(parts, axis=1), 0, 0)
        dqs = jnp.concatenate([dq_ref[g, cp].reshape(256, 128) for g in range(GROUPS)], axis=1)
        dwq = dwq + dot(xq[0, cp].reshape(256, 384), dqs, 0, 0)

    def put(at, value):
        dw_ref[:, at:at + value.shape[1]] = value if dw_in is None else value + dw_in[:, at:at + value.shape[1]]

    put(0, dwq)
    for g in range(GROUPS):
        put(384 + 128 * g, dw[:, 256 * g:256 * g + 128])
        put(768 + 128 * g, dw[:, 256 * g + 128:256 * g + 256])


def cross_kernel(rp, edge_ref, near_ref, far_ref, far_g_ref, near_stat, far_stat, kv, own_ref, w_ref, split_ref,
                 dkvs, xq, q, do, bias, sc, pd, rhs, acc, tail, stats):
    odd = edge_ref[2]
    stats[:, :, :, :, :128] = jnp.where(odd == 1, near_stat[...], far_stat[...])
    stats[:, :, :, :, 128:] = jnp.where(odd == 1, far_stat[...], near_stat[...])
    key = lax.broadcasted_iota(jnp.int32, (64, 256), 0)
    lane = lax.broadcasted_iota(jnp.int32, (64, 256), 1)
    krow, kcol, qrow = key // 16, key % 16, (lane % 32) // 8
    dcol = kcol - lane % 8
    ok = ((lane < 128) & (krow < qrow)) | ((lane >= 128) & (krow > qrow))
    ok = ok & (dcol >= 0) & (dcol <= 6)
    for which, extra in enumerate((kcol >= 3, kcol >= 0, kcol < 11)):
        bias[which] = jnp.where(ok & extra, 0.0, -1e30).astype(F32)
    pick, pick_b = head_masks()

    def side_patches(side, x_row, d_row):
        lines = [None, 0, 1, 2] if side == 0 else [0, 1, 2, None]
        for pair in range(2):
            rows = lines[2 * pair:2 * pair + 2]
            at = slice(16 * pair, 16 * pair + 16)

            def store_x(cp, p, block, at=at):
                xq[cp, p, at] = block

            def store_g(cp, p, block, at=at):
                for g in range(GROUPS):
                    do[side, g, cp, p, at] = block[:, 128 * g:128 * g + 128]

            to_patches([None if r is None else x_row(r) for r in rows], split_ref, store_x)
            to_patches([None if r is None else d_row(r) for r in rows], split_ref, store_g)
        for cp in range(2):
            qs = dot(xq[cp].reshape(256, 384), w_ref[:, :384]).astype(BF)
            for g in range(GROUPS):
                q[side, g, cp] = qs[:, 128 * g:128 * g + 128].reshape(8, 32, 128)

    for parity in range(2):
        @pl.when(odd == parity)
        def _(parity=parity):
            side_patches(1 - parity, lambda r: near_ref[0, r, rp], lambda r: near_ref[1, r, rp])
            side_patches(parity, lambda r: far_ref[r], lambda r: far_g_ref[r, rp])

    def attend(step, carry):
        def place_of(u):
            index = step * (CROSS_UNITS // 8) + u // 8
            return index // 2, (index % 2 if CROSS_UNITS == 8 else u // 8), u % 8

        def score(u):
            g, cp, p = place_of(u)
            slot = u % SLOTS
            for side in range(2):
                for h in range(4):
                    at = slice(128 * side + 32 * h, 128 * side + 32 * h + 32)
                    rhs[slot, 0, at] = q[side, g, cp, p] * pick_b[h]
                    rhs[slot, 1, at] = do[side, g, cp, p] * pick_b[h]
            keys = kv[0, g, cp, p].reshape(64, 256)
            for part in range(2):
                sc[u % (LAG + 1), part] = dot(keys[:, 128 * part:128 * part + 128], rhs[slot, part], 1, 1)

        def soften(u):
            g, cp, p = place_of(u)
            now = u % (LAG + 1)
            s = (sc[now, 0] + bias[edge_kind(p)]) * C
            att = jnp.exp2(s - stats[0, g, cp, p:p + 1])
            pd[now, 0] = (att * (sc[now, 1] - stats[1, g, cp, p:p + 1])).astype(BF)
            pd[now, 1] = att.astype(BF)

        def spread(u):
            g, cp, p = place_of(u)
            for part in range(2):
                lanes = slice(128 * part, 128 * part + 128)
                value = dot(pd[u % (LAG + 1), part], rhs[u % SLOTS, part]).reshape(4, 16, 128)
                head = value[:, :8] + own_ref[g, cp, :, 8 * p:8 * p + 8, lanes]
                if p > 0:
                    head = head + tail[(p + 1) % 2, :, :, lanes]
                acc[:, 8 * p:8 * p + 8, lanes] = head
                if p < 7:
                    tail[p % 2, :, :, lanes] = value[:, 8:]
                else:
                    acc[:, 64:72, lanes] = value[:, 8:] + own_ref[g, cp, :, 64:72, lanes]
            if p == 7:
                acc[:, 72:80, :] = jnp.zeros((4, 8, 256), F32)
                dkvs[g, cp, :, :, :128] = (acc[:, :, :128] * SCALE).astype(BF)
                dkvs[g, cp, :, :, 128:] = acc[:, :, 128:].astype(BF)

        for t in range(CROSS_UNITS + 2 * LAG):
            if t < CROSS_UNITS:
                score(t)
            if 0 <= t - LAG < CROSS_UNITS:
                soften(t - LAG)
            if 0 <= t - 2 * LAG < CROSS_UNITS:
                spread(t - 2 * LAG)
        return carry

    lax.fori_loop(0, 48 // CROSS_UNITS, attend, 0)


def final_kernel(dq0_ref, dq1_ref, dkv0_ref, dkv1_ref, w_ref, unplace_ref, unsplit_ref, out_ref):
    for rp, (dq_ref, dkvs) in enumerate(((dq0_ref, dkv0_ref), (dq1_ref, dkv1_ref))):
        for pair in range(2):
            quads = [jnp.concatenate([dq_ref[g, cp, p, 16 * pair:16 * pair + 16] for g in range(GROUPS)], axis=1).astype(F32)
                     for cp in range(2) for p in range(8)]
            for sub in range(2):
                kq = 2 * pair + sub
                dqs = jnp.concatenate([t[8 * sub:8 * sub + 8] for t in quads], axis=0).astype(BF)
                parts = [jnp.concatenate([dkvs[g, 0, kq], dkvs[g, 1, kq]], axis=0) for g in range(GROUPS)]
                both = jnp.concatenate([t[:, :128] for t in parts] + [t[:, 128:] for t in parts], axis=1)
                nq = dot(unsplit_ref[...], dqs).astype(BF)
                nkv = dot(unplace_ref[...], both).astype(BF)
                out_ref[2 * kq + rp] = dot(jnp.concatenate([nq, nkv], axis=1), w_ref[...], 1, 1).astype(BF)


def after(value, *others):
    return lax.optimization_barrier((value,) + others)[0]


def exchange(x, axis, dim, bit_count, low, behind):
    count = lax.axis_size(axis)
    span = 1 << bit_count
    mine = (lax.axis_index(axis) >> low) & (span - 1)
    total = lax.dynamic_index_in_dim(x, mine, dim, keepdims=False).astype(F32)
    sent = [lax.ppermute(lax.dynamic_index_in_dim(x, mine ^ turn, dim, keepdims=False).astype(BF), axis,
                         [(i, i ^ (turn << low)) for i in range(count)]) for turn in range(1, span)]
    for block in lax.optimization_barrier((behind, *sent))[1:]:
        total = total + block.astype(F32)
    return total


def block(shape, *at):
    at = at + (0,) * (len(shape) - len(at))
    return pl.BlockSpec(shape, lambda i: at)


def whole(x):
    return block(x.shape)


SMEM = pl.BlockSpec(memory_space=pltpu.SMEM)
ANY = pl.BlockSpec(memory_space=pl.ANY)


def call(kernel, name, us, outs, out_specs, scratch, args, in_specs, aliases={}):
    return pl.pallas_call(
        kernel,
        grid=(1,),
        out_shape=[jax.ShapeDtypeStruct(s, t) for s, t in outs],
        in_specs=in_specs,
        out_specs=out_specs,
        scratch_shapes=[pltpu.VMEM(s, t) for s, t in scratch],
        compiler_params=pltpu.CompilerParams(vmem_limit_bytes=VMEM_BYTES),
        cost_estimate=pl.CostEstimate(flops=int(us * 1e9), bytes_accessed=1 << 20, transcendentals=0),
        input_output_aliases=aliases,
        name=name,
    )(*args)


def pack_call(edge, x4, g4):
    rows = x4.shape[2:]
    return pl.pallas_call(
        pack_kernel,
        out_shape=[jax.ShapeDtypeStruct(s + rows, BF) for s in ((3,), (3,), (3, 2), (2, 3, 2))],
        in_specs=[SMEM, ANY, ANY],
        out_specs=[ANY] * 4,
        scratch_shapes=[pltpu.VMEM(x4.shape, BF), pltpu.VMEM(g4.shape, BF), pltpu.SemaphoreType.DMA((7,))],
        name="pack",
    )(edge, x4, g4)


def own_call(x4, g4, w, place, split):
    outs = [((2, 3, 2, 8, 32, 128), BF), ((2, 3, 2, 8, 32, 128), BF), ((2, 2, 8, 32, 384), BF),
            ((2, 3, 2, 8, 4, 16, 256), BF), ((2, 2, 4, 80, 384), BF)]
    args = (x4, g4, w, place, split)
    return call(own_kernel, "own", 4, outs, [block(s) for s, _ in outs], [((384, 768), BF)], args, [whole(a) for a in args])


def attend_call(rp, edge, near, far, q, do, xq, kv, xk, w, place, dw):
    def kernel(*refs):
        attend_kernel(rp, *refs)

    outs = [((3, 2, 8, 32, 128), BF), ((3, 2, 4, 80, 256), F32), ((2, 3, 2, 8, 128), F32), ((384, 1152), F32)]
    args = [edge, near, far, q, do, xq, kv, xk, w, place]
    specs = [SMEM, whole(near), whole(far)] + [block((1,) + a.shape[1:], rp) for a in (q, do, xq, kv, xk)] + [whole(w), whole(place)]
    if rp == 1:
        args.append(dw)
        specs.append(whole(dw))
    return call(kernel, "attend", 12, outs, [block(s) for s, _ in outs], [
        ((2, 6, 80, 384), BF), ((3, 2, 8, 6, 16, 256), BF), ((3, 2, 6, 80, 256), F32), ((3, 160, 128), F32),
        ((384, 768), BF), ((LAG + 1, 160, 256), F32), ((LAG + 1, 160, 256), BF), ((SLOTS, 256, 256), BF), ((2, 10, 8, 256), F32),
    ], args, specs)


def cross_call(rp, edge, near, far, far_g, stat_near, stat_far, kv, own, w, split):
    def kernel(*refs):
        cross_kernel(rp, *refs)

    args = [edge, near, far, far_g, stat_near, stat_far, kv, own, w, split]
    specs = [SMEM] + [whole(a) for a in args[1:6]] + [block((1,) + kv.shape[1:], rp)] + [whole(a) for a in args[7:]]
    return call(kernel, "cross", 9, [((3, 2, 4, 80, 256), BF)], [block((3, 2, 4, 80, 256))], [
        ((2, 8, 32, 384), BF), ((2, 3, 2, 8, 32, 128), BF), ((2, 3, 2, 8, 32, 128), BF),
        ((3, 64, 256), F32), ((LAG + 1, 2, 64, 256), F32), ((LAG + 1, 2, 64, 256), BF), ((SLOTS, 2, 256, 128), BF),
        ((4, 80, 256), F32), ((2, 4, 8, 256), F32), ((2, 3, 2, 8, 256), F32),
    ], args, specs)[0]


def final_call(shape, *args):
    return call(final_kernel, "final", 4, [(shape, BF)], [block(shape)], [], args, [whole(a) for a in args])[0]


def shards(features, qkv_weight, grad_output):
    row_count, col_count, width = features.shape
    count = lax.axis_size("row")
    index = lax.axis_index("row")
    odd = index & 1
    near = [(i, i ^ 1) for i in range(count)]
    far = [(i, i + 1) for i in range(1, count - 1, 2)] + [(i + 1, i) for i in range(1, count - 1, 2)]
    place, split = column_maps()
    edge = jnp.stack([jnp.where(index == 0, 3, 0), jnp.where(index == count - 1, 7, 10), odd]).astype(jnp.int32)
    x4, g4 = (a.reshape(row_count // 2, 2, col_count, width) for a in (features, grad_output))
    send_x0, send_x1, send_g, send_near = pack_call(edge, x4, g4)

    far_x0 = lax.ppermute(send_x0, "row", far)
    near_xg = lax.ppermute(send_near, "row", near)
    q, do, xq, kv, xk = own_call(x4, g4, qkv_weight, place, split)
    far_x1 = lax.ppermute(after(send_x1, far_x0, xk), "row", far)
    dq0, own0, stat0, dw0 = attend_call(0, edge, near_xg, far_x0, q, do, xq, kv, xk, qkv_weight, place, None)
    far_x1 = after(far_x1, dw0)
    far_g = lax.ppermute(after(send_g, far_x1), "row", far)
    stat0_near = lax.ppermute(stat0, "row", near)
    stat0_far = lax.ppermute(stat0, "row", far)
    dq1, own1, stat1, dw1 = attend_call(1, edge, near_xg, far_x1, q, do, xq, kv, xk, qkv_weight, place, dw0)
    far_g, stat0_near, stat0_far, _ = lax.optimization_barrier((far_g, stat0_near, stat0_far, dq1))
    stat1_near = lax.ppermute(stat1, "row", near)
    stat1_far = lax.ppermute(stat1, "row", far)
    bits = count.bit_length() - 1
    rows = width // count
    dkv0 = cross_call(0, edge, near_xg, far_x0, far_g, stat0_near, stat0_far, kv, own0, qkv_weight, split)
    stat1_near, stat1_far, _ = lax.optimization_barrier((stat1_near, stat1_far, dkv0))
    total = exchange(dw1.reshape(count // 2, 2, rows, 3 * width), "row", 1, 1, 0, dkv0)
    dkv1 = cross_call(1, edge, near_xg, far_x1, far_g, stat1_near, stat1_far, kv, own1, qkv_weight, split)
    total = exchange(total.reshape(count // 4, 2, rows, 3 * width), "row", 1, 1, 1, dkv1)
    grad_features = final_call(features.shape, dq0, dq1, dkv0, dkv1, qkv_weight, place.T, split.T)
    low = 2
    while low < bits:
        step = min(2, bits - low)
        total = exchange(total.reshape(count >> (low + step), 1 << step, rows, 3 * width), "row", 1, step, low, grad_features)
        low += step
    grad_weight = total.reshape(rows, 3 * width) * (row_count * count * col_count) ** -0.5
    return grad_features, grad_weight


def solution(mesh):
    placed = (P(("group", "row"), None, None), P(), P(("group", "row"), None, None))
    return jax.shard_map(
        shards,
        mesh=mesh,
        in_specs=placed,
        out_specs=(P(("group", "row"), None, None), P(("group", "row"), None)),
        check_vma=False,
    )
```

```python
import jax
import jax.numpy as jnp
import numpy as np
from jax import lax
from jax.experimental import pallas as pl
from jax.experimental.pallas import tpu as pltpu
from jax.sharding import PartitionSpec as P

HEADS = 12
WINDOW = 7
DILATION = 2
HALO = 6
GROUPS = 3
UNITS = 48
LAG = 3
SLOTS = 2 * LAG + 1
CROSS_UNITS = 48
BF = jnp.bfloat16
F32 = jnp.float32
SCALE = 32 ** -0.5
C = SCALE * 1.4426950408889634
VMEM_BYTES = 40 << 20


def dot(a, b, ca=1, cb=0):
    return lax.dot_general(a, b, (((ca,), (cb,)), ((), ())), preferred_element_type=F32)


def column_maps():
    place = np.zeros((160, 128), np.float32)
    split = np.zeros((128, 128), np.float32)
    for col in range(128):
        place[80 * (col % 2) + col // 2 + 3, col] = 1
        split[64 * (col % 2) + col // 2, col] = 1
    return jnp.asarray(place, BF), jnp.asarray(split, BF)


def gather_kv_weight(w_ref, wkv):
    for g in range(GROUPS):
        wkv[:, 256 * g:256 * g + 128] = w_ref[:, 384 + 128 * g:384 + 128 * g + 128]
        wkv[:, 256 * g + 128:256 * g + 256] = w_ref[:, 768 + 128 * g:768 + 128 * g + 128]


def project_keys(x, place_ref, wkv, xk, kv, k):
    placed = dot(place_ref[...], x).astype(BF)
    xk[0, k] = placed[:80]
    xk[1, k] = placed[80:]
    both = dot(placed, wkv[...])
    for cp in range(2):
        for p in range(8):
            block = both[80 * cp + 8 * p:80 * cp + 8 * p + 16].astype(BF)
            for g in range(GROUPS):
                kv[g, cp, p, k] = block[:, 256 * g:256 * g + 256]


def to_patches(pair_rows, split_ref, store):
    parts = [None if row is None else dot(split_ref[...], row) for row in pair_rows]
    for cp in range(2):
        for p in range(8):
            at = slice(64 * cp + 8 * p, 64 * cp + 8 * p + 8)
            known = [part for part in parts if part is not None][0][at]
            halves = [jnp.zeros_like(known) if part is None else part[at] for part in parts]
            store(cp, p, jnp.concatenate(halves, axis=0).astype(BF))


def first_kernel(x_ref, x0_ref, xs, sem):
    odd = lax.axis_index("row") & 1
    load = pltpu.make_async_copy(x_ref.at[pl.ds(odd, 3), 0], xs, sem.at[0])
    load.start()
    load.wait()
    store = pltpu.make_async_copy(xs, x0_ref, sem.at[1])
    store.start()
    store.wait()


def pack_kernel(first_ref, x_ref, g_ref, x1_ref, fg_ref, near_ref, xs, gs, sem):
    odd = lax.axis_index("row") & 1
    mine, other = pl.ds(odd, 3), pl.ds(1 - odd, 3)
    loads = [pltpu.make_async_copy(x_ref, xs, sem.at[0]), pltpu.make_async_copy(g_ref, gs, sem.at[1])]
    for copy in loads:
        copy.start()
    loads[0].wait()
    copies = [
        pltpu.make_async_copy(xs.at[other], near_ref.at[0], sem.at[2]),
        pltpu.make_async_copy(xs.at[mine, 1], x1_ref, sem.at[3]),
        pltpu.make_async_copy(gs.at[other], near_ref.at[1], sem.at[4]),
        pltpu.make_async_copy(gs.at[mine], fg_ref, sem.at[5]),
    ]
    for copy in copies[:2]:
        copy.start()
    loads[1].wait()
    for copy in copies[2:]:
        copy.start()
    for copy in copies:
        copy.wait()


def own_kernel(*refs):
    sources, (q_ref, g_ref, xq_ref, kv_ref, xk_ref, wkv), held, sem = refs[:5], refs[5:11], refs[11:16], refs[16]
    loads = [pltpu.make_async_copy(source, room, sem.at[n]) for n, (source, room) in enumerate(zip(sources, held))]
    for copy in loads:
        copy.start()
    for copy in loads:
        copy.wait()
    x_ref, do_ref, w_ref, place_ref, split_ref = held
    gather_kv_weight(w_ref, wkv)
    for rp in range(2):
        for k in range(4):
            project_keys(x_ref[k, rp], place_ref, wkv, xk_ref.at[rp], kv_ref.at[rp], k)
        for pair in range(2):
            at = slice(16 * pair, 16 * pair + 16)

            def store_x(cp, p, block, at=at, rp=rp):
                xq_ref[rp, cp, p, at] = block

            def store_g(cp, p, block, at=at, rp=rp):
                for g in range(GROUPS):
                    g_ref[rp, g, cp, p, at] = block[:, 128 * g:128 * g + 128]

            to_patches([x_ref[2 * pair + d, rp] for d in range(2)], split_ref, store_x)
            to_patches([do_ref[2 * pair + d, rp] for d in range(2)], split_ref, store_g)
        for cp in range(2):
            qs = dot(xq_ref[rp, cp].reshape(256, 384), w_ref[:, :384]).astype(BF)
            for g in range(GROUPS):
                q_ref[rp, g, cp] = qs[:, 128 * g:128 * g + 128].reshape(8, 32, 128)


def window_bias(bias, key_rows, row_ok):
    shape = (16 * key_rows, 128)
    key = lax.broadcasted_iota(jnp.int32, shape, 0)
    lane = lax.broadcasted_iota(jnp.int32, shape, 1)
    krow, kcol = key // 16, key % 16
    qrow, dcol = (lane % 32) // 8, key % 16 - lane % 8
    ok = row_ok(krow, qrow) & (dcol >= 0) & (dcol <= 6)
    for which, extra in enumerate((kcol >= 3, kcol >= 0, kcol < 11)):
        bias[which] = jnp.where(ok & extra, 0.0, -1e30).astype(F32)


def head_masks():
    head_lane = lax.broadcasted_iota(jnp.int32, (32, 128), 1) // 32
    return [head_lane == h for h in range(4)], [(head_lane == h).astype(F32).astype(BF) for h in range(4)]


def pack_heads(rhs, slot, qp, gp, pick_b):
    for h in range(4):
        rhs[slot, 32 * h:32 * h + 32, :128] = qp * pick_b[h]
        rhs[slot, 128 + 32 * h:160 + 32 * h, 128:] = gp * pick_b[h]


def clear_off_diagonal(rhs):
    for slot in range(rhs.shape[0]):
        rhs[slot, :128, 128:] = jnp.zeros((128, 128), BF)
        rhs[slot, 128:, :128] = jnp.zeros((128, 128), BF)


def edge_kind(p):
    return 0 if p == 0 else (2 if p == 7 else 1)


def attend_kernel(rp, near_ref, far_ref, q, do, xq, kv, xk, w_ref, place_ref, *refs):
    if rp == 0:
        send_ref, gs_ref, *refs = refs
        gs_ref[:768] = send_ref[...].reshape(768, 384)
    dq_ref, own_ref, stat_ref, dw_ref, xh, kvh, acc, bias, wkv, sc, pd, rhs, tail = refs
    index = lax.axis_index("row")
    odd = index & 1
    low = jnp.where(index == 0, 3, 0)
    high = jnp.where(index == lax.axis_size("row") - 1, 7, 10)
    gather_kv_weight(w_ref, wkv)
    window_bias(bias, 10, lambda krow, qrow: (krow >= qrow) & (krow <= qrow + 6) & (krow >= low) & (krow < high))

    for k in range(3):
        project_keys(near_ref[0, k, rp], place_ref, wkv, xh, kvh, k + 3 - 3 * odd)
    for k in range(3):
        project_keys(far_ref[k], place_ref, wkv, xh, kvh, k + 3 * odd)
    pick, pick_b = head_masks()
    clear_off_diagonal(rhs)

    def attend(step, carry):
        def place_of(u):
            index = step * (UNITS // 8) + u // 8
            return index // 2, (u // 8) % 2, u % 8

        def keys(u):
            g, cp, p = place_of(u)
            return jnp.concatenate([
                kvh[g, cp, p, :3].reshape(48, 256),
                kv[rp, g, cp, p].reshape(64, 256),
                kvh[g, cp, p, 3:].reshape(48, 256)], axis=0)

        def score(u):
            g, cp, p = place_of(u)
            pack_heads(rhs, u % SLOTS, q[rp, g, cp, p], do[rp, g, cp, p], pick_b)
            sc[u % (LAG + 1)] = dot(keys(u), rhs[u % SLOTS], 1, 1)

        def soften(u):
            g, cp, p = place_of(u)
            now, slot = u % (LAG + 1), u % (LAG + 1)
            s = sc[now, :, :128] + bias[edge_kind(p)]
            m = jnp.max(s, axis=0, keepdims=True)
            e = jnp.exp2((s - m) * C)
            dp = sc[now, :, 128:]
            total = jnp.sum(e, axis=0, keepdims=True)
            inv = 1.0 / total
            delta = jnp.sum(e * dp, axis=0, keepdims=True) * inv
            att = e * inv
            pd[slot, :, :128] = (att * (dp - delta)).astype(BF)
            pd[slot, :, 128:] = att.astype(BF)
            stat_ref[0, g, cp, p:p + 1] = m * C + jnp.log2(total)
            stat_ref[1, g, cp, p:p + 1] = delta

        def spread(u):
            g, cp, p = place_of(u)
            slot = u % (LAG + 1)

            def add_to(at, value):
                acc[g, cp, :3, at, :] = value[:3]
                own_ref[g, cp, :, at, :] = value[3:7]
                acc[g, cp, 3:, at, :] = value[7:]

            dkv = dot(pd[slot], rhs[u % SLOTS]).reshape(10, 16, 256)
            head = dkv[:, :8]
            if p > 0:
                head = head + tail[(p + 1) % 2]
            add_to(slice(8 * p, 8 * p + 8), head)
            if p < 7:
                tail[p % 2] = dkv[:, 8:]
            else:
                add_to(slice(64, 72), dkv[:, 8:])
                add_to(slice(72, 80), jnp.zeros((10, 8, 256), F32))
            full = dot(pd[slot, :, :128], keys(u)[:, :128], 0, 0)
            dq = jnp.where(pick[3], full[96:], 0.0)
            for h in range(3):
                dq = jnp.where(pick[h], full[32 * h:32 * h + 32], dq)
            dq_ref[g, cp, p] = (dq * SCALE).astype(BF)

        for t in range(UNITS + 2 * LAG):
            if t < UNITS:
                score(t)
            if 0 <= t - LAG < UNITS:
                soften(t - LAG)
            if 0 <= t - 2 * LAG < UNITS:
                spread(t - 2 * LAG)
        return carry

    if UNITS == 48:
        attend(0, 0)
    else:
        lax.fori_loop(0, 48 // UNITS, attend, 0)
    if rp == 0:
        rest = stat_ref[...].reshape(96, 128)
        for part in range(3):
            piece = rest.astype(BF)
            gs_ref[768:, 128 * part:128 * part + 128] = piece
            rest = rest - piece.astype(F32)

    dw = jnp.zeros((384, 768), F32)
    dwq = jnp.zeros((384, 384), F32)
    for cp in range(2):
        for xs, ref, n in ((xh[cp], acc, 480), (xk[rp, cp], own_ref, 320)):
            parts = []
            for g in range(GROUPS):
                a = ref[g, cp].reshape(n, 256)
                parts.append((a[:, :128] * SCALE).astype(BF))
                parts.append(a[:, 128:].astype(BF))
            dw = dw + dot(xs.reshape(n, 384), jnp.concatenate(parts, axis=1), 0, 0)
        dqs = jnp.concatenate([dq_ref[g, cp].reshape(256, 128) for g in range(GROUPS)], axis=1)
        dwq = dwq + dot(xq[rp, cp].reshape(256, 384), dqs, 0, 0)

    dw_ref[:, :384] = dwq
    for g in range(GROUPS):
        dw_ref[:, 384 + 128 * g:512 + 128 * g] = dw[:, 256 * g:256 * g + 128]
        dw_ref[:, 768 + 128 * g:896 + 128 * g] = dw[:, 256 * g + 128:256 * g + 256]


def cross_kernel(rp, near_ref, far_ref, far_gs_ref, near_stat, far_stat, kv, own_ref, w_ref, split_ref,
                 dkvs, xq, q, do, bias, sc, pd, rhs, acc, tail, stats):
    odd = lax.axis_index("row") & 1
    if far_stat is None:
        parts = far_gs_ref[768:].astype(F32)
        far_rows = (parts[:, :128] + parts[:, 128:256] + parts[:, 256:]).reshape(near_stat.shape)
    else:
        far_rows = far_stat[...]
    stats[:, :, :, :, :128] = jnp.where(odd == 1, near_stat[...], far_rows)
    stats[:, :, :, :, 128:] = jnp.where(odd == 1, far_rows, near_stat[...])
    key = lax.broadcasted_iota(jnp.int32, (64, 256), 0)
    lane = lax.broadcasted_iota(jnp.int32, (64, 256), 1)
    krow, kcol, qrow = key // 16, key % 16, (lane % 32) // 8
    dcol = kcol - lane % 8
    ok = ((lane < 128) & (krow < qrow)) | ((lane >= 128) & (krow > qrow))
    ok = ok & (dcol >= 0) & (dcol <= 6)
    for which, extra in enumerate((kcol >= 3, kcol >= 0, kcol < 11)):
        bias[which] = jnp.where(ok & extra, 0.0, -1e30).astype(F32)
    pick, pick_b = head_masks()

    def side_patches(side, x_row, d_row):
        lines = [None, 0, 1, 2] if side == 0 else [0, 1, 2, None]
        for pair in range(2):
            rows = lines[2 * pair:2 * pair + 2]
            at = slice(16 * pair, 16 * pair + 16)

            def store_x(cp, p, block, at=at):
                xq[cp, p, at] = block

            def store_g(cp, p, block, at=at):
                for g in range(GROUPS):
                    do[side, g, cp, p, at] = block[:, 128 * g:128 * g + 128]

            to_patches([None if r is None else x_row(r) for r in rows], split_ref, store_x)
            to_patches([None if r is None else d_row(r) for r in rows], split_ref, store_g)
        for cp in range(2):
            qs = dot(xq[cp].reshape(256, 384), w_ref[:, :384]).astype(BF)
            for g in range(GROUPS):
                q[side, g, cp] = qs[:, 128 * g:128 * g + 128].reshape(8, 32, 128)

    for parity in range(2):
        @pl.when(odd == parity)
        def _(parity=parity):
            side_patches(1 - parity, lambda r: near_ref[0, r, rp], lambda r: near_ref[1, r, rp])
            side_patches(parity, lambda r: far_ref[r], lambda r: far_gs_ref[256 * r + 128 * rp:256 * r + 128 * rp + 128])

    def attend(step, carry):
        def place_of(u):
            index = step * (CROSS_UNITS // 8) + u // 8
            return index // 2, (u // 8) % 2, u % 8

        def score(u):
            g, cp, p = place_of(u)
            slot = u % SLOTS
            for side in range(2):
                for h in range(4):
                    at = slice(128 * side + 32 * h, 128 * side + 32 * h + 32)
                    rhs[slot, 0, at] = q[side, g, cp, p] * pick_b[h]
                    rhs[slot, 1, at] = do[side, g, cp, p] * pick_b[h]
            keys = kv[rp, g, cp, p].reshape(64, 256)
            for part in range(2):
                sc[u % (LAG + 1), part] = dot(keys[:, 128 * part:128 * part + 128], rhs[slot, part], 1, 1)

        def soften(u):
            g, cp, p = place_of(u)
            now = u % (LAG + 1)
            s = (sc[now, 0] + bias[edge_kind(p)]) * C
            att = jnp.exp2(s - stats[0, g, cp, p:p + 1])
            pd[now, 0] = (att * (sc[now, 1] - stats[1, g, cp, p:p + 1])).astype(BF)
            pd[now, 1] = att.astype(BF)

        def spread(u):
            g, cp, p = place_of(u)
            for part in range(2):
                lanes = slice(128 * part, 128 * part + 128)
                value = dot(pd[u % (LAG + 1), part], rhs[u % SLOTS, part]).reshape(4, 16, 128)
                head = value[:, :8] + own_ref[g, cp, :, 8 * p:8 * p + 8, lanes]
                if p > 0:
                    head = head + tail[(p + 1) % 2, :, :, lanes]
                acc[:, 8 * p:8 * p + 8, lanes] = head
                if p < 7:
                    tail[p % 2, :, :, lanes] = value[:, 8:]
                else:
                    acc[:, 64:72, lanes] = value[:, 8:] + own_ref[g, cp, :, 64:72, lanes]
            if p == 7:
                acc[:, 72:80, :] = jnp.zeros((4, 8, 256), F32)
                dkvs[g, cp, :, :, :128] = (acc[:, :, :128] * SCALE).astype(BF)
                dkvs[g, cp, :, :, 128:] = acc[:, :, 128:].astype(BF)

        for t in range(CROSS_UNITS + 2 * LAG):
            if t < CROSS_UNITS:
                score(t)
            if 0 <= t - LAG < CROSS_UNITS:
                soften(t - LAG)
            if 0 <= t - 2 * LAG < CROSS_UNITS:
                spread(t - 2 * LAG)
        return carry

    if CROSS_UNITS == 48:
        attend(0, 0)
    else:
        lax.fori_loop(0, 48 // CROSS_UNITS, attend, 0)


def final_kernel(dq0_ref, dq1_ref, dkv0_ref, dkv1_ref, w_ref, unplace_ref, unsplit_ref, out_ref):
    for rp, (dq_ref, dkvs) in enumerate(((dq0_ref, dkv0_ref), (dq1_ref, dkv1_ref))):
        for pair in range(2):
            quads = [jnp.concatenate([dq_ref[g, cp, p, 16 * pair:16 * pair + 16] for g in range(GROUPS)], axis=1).astype(F32)
                     for cp in range(2) for p in range(8)]
            for sub in range(2):
                kq = 2 * pair + sub
                dqs = jnp.concatenate([t[8 * sub:8 * sub + 8] for t in quads], axis=0).astype(BF)
                parts = [jnp.concatenate([dkvs[g, 0, kq], dkvs[g, 1, kq]], axis=0) for g in range(GROUPS)]
                both = jnp.concatenate([t[:, :128] for t in parts] + [t[:, 128:] for t in parts], axis=1)
                nq = dot(unsplit_ref[...], dqs).astype(BF)
                nkv = dot(unplace_ref[...], both).astype(BF)
                out_ref[2 * kq + rp] = dot(jnp.concatenate([nq, nkv], axis=1), w_ref[...], 1, 1).astype(BF)


def after(value, *others):
    return lax.optimization_barrier((value,) + others)[0]


def exchange(x, axis, dim, bit_count, low, behind):
    count = lax.axis_size(axis)
    span = 1 << bit_count
    mine = (lax.axis_index(axis) >> low) & (span - 1)
    total = lax.dynamic_index_in_dim(x, mine, dim, keepdims=False).astype(F32)
    sent = [lax.ppermute(lax.dynamic_index_in_dim(x, mine ^ turn, dim, keepdims=False).astype(BF), axis,
                         [(i, i ^ (turn << low)) for i in range(count)]) for turn in range(1, span)]
    for block in lax.optimization_barrier((behind, *sent))[1:]:
        total = total + block.astype(F32)
    return total


VM = pl.BlockSpec(memory_space=pltpu.VMEM)
ANY = pl.BlockSpec(memory_space=pl.ANY)


def call(kernel, name, us, outs, scratch, args):
    return pl.pallas_call(
        kernel,
        out_shape=[jax.ShapeDtypeStruct(s, t) for s, t in outs],
        in_specs=[VM] * len(args),
        out_specs=[VM] * len(outs),
        scratch_shapes=[pltpu.VMEM(s, t) for s, t in scratch],
        compiler_params=pltpu.CompilerParams(vmem_limit_bytes=VMEM_BYTES),
        cost_estimate=pl.CostEstimate(flops=int(us * 1e9), bytes_accessed=1 << 20, transcendentals=0),
        name=name,
    )(*args)


def raw_call(kernel, name, outs, scratch, args):
    return pl.pallas_call(
        kernel,
        out_shape=[jax.ShapeDtypeStruct(s, BF) for s in outs],
        in_specs=[ANY] * len(args),
        out_specs=[ANY] * len(outs),
        scratch_shapes=[pltpu.VMEM(s, BF) for s in scratch] + [pltpu.SemaphoreType.DMA((6,))],
        name=name,
    )(*args)


def own_call(*args):
    outs = [(2, 3, 2, 8, 32, 128), (2, 3, 2, 8, 32, 128), (2, 2, 8, 32, 384), (2, 3, 2, 8, 4, 16, 256), (2, 2, 4, 80, 384)]
    return pl.pallas_call(
        own_kernel,
        out_shape=[jax.ShapeDtypeStruct(s, BF) for s in outs],
        in_specs=[ANY] * len(args),
        out_specs=[VM] * len(outs),
        scratch_shapes=[pltpu.VMEM((384, 768), BF)] + [pltpu.VMEM(a.shape, BF) for a in args] + [pltpu.SemaphoreType.DMA((5,))],
        compiler_params=pltpu.CompilerParams(vmem_limit_bytes=VMEM_BYTES),
        cost_estimate=pl.CostEstimate(flops=4000000000, bytes_accessed=1 << 20, transcendentals=0),
        name="own",
    )(*args)


def attend_call(rp, *args):
    def kernel(*refs):
        attend_kernel(rp, *refs)

    outs = [((3, 2, 8, 32, 128), BF), ((3, 2, 4, 80, 256), F32), ((2, 3, 2, 8, 128), F32), ((384, 1152), F32)]
    if rp == 0:
        outs = [((864, 384), BF)] + outs
    return call(kernel, "attend", 10, outs, [
        ((2, 6, 80, 384), BF), ((3, 2, 8, 6, 16, 256), BF), ((3, 2, 6, 80, 256), F32), ((3, 160, 128), F32),
        ((384, 768), BF), ((LAG + 1, 160, 256), F32), ((LAG + 1, 160, 256), BF), ((SLOTS, 256, 256), BF), ((2, 10, 8, 256), F32),
    ], args)


def cross_call(rp, near, far, far_gs, stat_near, stat_far, kv, own, w, split):
    args = [near, far, far_gs, stat_near, stat_far, kv, own, w, split]
    if rp == 0:
        del args[4]

    def kernel(*refs):
        refs = list(refs)
        if rp == 0:
            refs.insert(4, None)
        cross_kernel(rp, *refs)

    return call(kernel, "cross", 6, [((3, 2, 4, 80, 256), BF)], [
        ((2, 8, 32, 384), BF), ((2, 3, 2, 8, 32, 128), BF), ((2, 3, 2, 8, 32, 128), BF),
        ((3, 64, 256), F32), ((LAG + 1, 2, 64, 256), F32), ((LAG + 1, 2, 64, 256), BF), ((SLOTS, 2, 256, 128), BF),
        ((4, 80, 256), F32), ((2, 4, 8, 256), F32), ((2, 3, 2, 8, 256), F32),
    ], args)[0]


def final_call(shape, *args):
    return call(final_kernel, "final", 4, [(shape, BF)], [], args)[0]


def shards(features, qkv_weight, grad_output):
    row_count, col_count, width = features.shape
    count = lax.axis_size("row")
    near = [(i, i ^ 1) for i in range(count)]
    far = [(i, i + 1) for i in range(1, count - 1, 2)] + [(i + 1, i) for i in range(1, count - 1, 2)]
    place, split = column_maps()
    x4, g4 = (a.reshape(row_count // 2, 2, col_count, width) for a in (features, grad_output))
    rim = (col_count, width)
    send_x0 = raw_call(first_kernel, "first", [(3,) + rim], [(3,) + rim], (x4,))[0]
    far_x0 = lax.ppermute(send_x0, "row", far)
    send_x1, send_g, send_near = raw_call(pack_kernel, "pack", [(3,) + rim, (3, 2) + rim, (2, 3, 2) + rim],
                                          [x4.shape, g4.shape], (send_x0, x4, g4))
    near_xg = lax.ppermute(send_near, "row", near)
    q, do, xq, kv, xk = own_call(x4, g4, qkv_weight, place, split)
    far_x1 = lax.ppermute(after(send_x1, far_x0, xk), "row", far)
    gs, dq0, own0, stat0, dw0 = attend_call(0, near_xg, far_x0, q, do, xq, kv, xk, qkv_weight, place, send_g)
    far_x1 = after(far_x1, dw0)
    far_gs = lax.ppermute(after(gs, far_x1), "row", far)
    stat0_near = lax.ppermute(stat0, "row", near)
    dq1, own1, stat1, dw1 = attend_call(1, near_xg, far_x1, q, do, xq, kv, xk, qkv_weight, place)
    far_gs, stat0_near, _ = lax.optimization_barrier((far_gs, stat0_near, dq1))
    stat1_near = lax.ppermute(stat1, "row", near)
    stat1_far = lax.ppermute(stat1, "row", far)
    bits = count.bit_length() - 1
    rows = width // count
    dkv0 = cross_call(0, near_xg, far_x0, far_gs, stat0_near, None, kv, own0, qkv_weight, split)
    stat1_near, stat1_far, _ = lax.optimization_barrier((stat1_near, stat1_far, dkv0))
    total = exchange((dw0 + dw1).reshape(count // 2, 2, rows, 3 * width), "row", 1, 1, 0, dkv0)
    dkv1 = cross_call(1, near_xg, far_x1, far_gs, stat1_near, stat1_far, kv, own1, qkv_weight, split)
    total = exchange(total.reshape(count // 4, 2, rows, 3 * width), "row", 1, 1, 1, dkv1)
    grad_features = final_call(features.shape, dq0, dq1, dkv0, dkv1, qkv_weight, place.T, split.T)
    low = 2
    while low < bits:
        step = min(2, bits - low)
        total = exchange(total.reshape(count >> (low + step), 1 << step, rows, 3 * width), "row", 1, step, low, grad_features)
        low += step
    grad_weight = total.reshape(rows, 3 * width) * (row_count * count * col_count) ** -0.5
    return grad_features, grad_weight


def solution(mesh):
    placed = (P(("group", "row"), None, None), P(), P(("group", "row"), None, None))
    return jax.shard_map(
        shards,
        mesh=mesh,
        in_specs=placed,
        out_specs=(P(("group", "row"), None, None), P(("group", "row"), None)),
        check_vma=False,
    )
```

```python
import jax
import jax.numpy as jnp
import numpy as np
from jax import lax
from jax.experimental import pallas as pl
from jax.experimental.pallas import tpu as pltpu
from jax.sharding import PartitionSpec as P

HEADS = 12
WINDOW = 7
DILATION = 2
HALO = 6
GROUPS = 3
UNITS = 48
LAG = 3
SLOTS = 2 * LAG + 1
CROSS_UNITS = 48
BF = jnp.bfloat16
F32 = jnp.float32
SCALE = 32 ** -0.5
C = SCALE * 1.4426950408889634
VMEM_BYTES = 40 << 20


def dot(a, b, ca=1, cb=0):
    return lax.dot_general(a, b, (((ca,), (cb,)), ((), ())), preferred_element_type=F32)


def column_maps():
    place = np.zeros((160, 128), np.float32)
    split = np.zeros((128, 128), np.float32)
    for col in range(128):
        place[80 * (col % 2) + col // 2 + 3, col] = 1
        split[64 * (col % 2) + col // 2, col] = 1
    return jnp.asarray(place, BF), jnp.asarray(split, BF)


def gather_kv_weight(w_ref, wkv):
    for g in range(GROUPS):
        wkv[:, 256 * g:256 * g + 128] = w_ref[:, 384 + 128 * g:384 + 128 * g + 128]
        wkv[:, 256 * g + 128:256 * g + 256] = w_ref[:, 768 + 128 * g:768 + 128 * g + 128]


def project_keys(x, place_ref, wkv, xk, kv, k):
    placed = dot(place_ref[...], x).astype(BF)
    xk[0, k] = placed[:80]
    xk[1, k] = placed[80:]
    both = dot(placed, wkv[...])
    for cp in range(2):
        for p in range(8):
            block = both[80 * cp + 8 * p:80 * cp + 8 * p + 16].astype(BF)
            for g in range(GROUPS):
                kv[g, cp, p, k] = block[:, 256 * g:256 * g + 256]


def to_patches(pair_rows, split_ref, store):
    parts = [None if row is None else dot(split_ref[...], row) for row in pair_rows]
    for cp in range(2):
        for p in range(8):
            at = slice(64 * cp + 8 * p, 64 * cp + 8 * p + 8)
            known = [part for part in parts if part is not None][0][at]
            halves = [jnp.zeros_like(known) if part is None else part[at] for part in parts]
            store(cp, p, jnp.concatenate(halves, axis=0).astype(BF))


def pack_kernel(x_ref, g_ref, x0_ref, near_ref, x1_ref, fg_ref, x0, near, x1, fg, sem):
    odd = lax.axis_index("row") & 1
    mine, other = pl.ds(odd, 3), pl.ds(1 - odd, 3)
    moves = [
        (x_ref.at[mine, 0], x0, x0_ref),
        (x_ref.at[other], near.at[0], near_ref.at[0]),
        (g_ref.at[other], near.at[1], near_ref.at[1]),
        (x_ref.at[mine, 1], x1, x1_ref),
        (g_ref.at[mine], fg, fg_ref),
    ]
    loads = [pltpu.make_async_copy(source, room, sem.at[n]) for n, (source, room, target) in enumerate(moves)]
    stores = [pltpu.make_async_copy(room, target, sem.at[5 + n]) for n, (source, room, target) in enumerate(moves)]
    for copy in loads:
        copy.start()
    for load, store in zip(loads, stores):
        load.wait()
        store.start()
    for copy in stores:
        copy.wait()


def own_kernel(*refs):
    sources, (q_ref, g_ref, xq_ref, kv_ref, xk_ref, wkv), held, sem = refs[:5], refs[5:11], refs[11:16], refs[16]
    loads = [pltpu.make_async_copy(source, room, sem.at[n]) for n, (source, room) in enumerate(zip(sources, held))]
    for copy in loads:
        copy.start()
    for copy in loads:
        copy.wait()
    x_ref, do_ref, w_ref, place_ref, split_ref = held
    gather_kv_weight(w_ref, wkv)
    for rp in range(2):
        for k in range(4):
            project_keys(x_ref[k, rp], place_ref, wkv, xk_ref.at[rp], kv_ref.at[rp], k)
        for pair in range(2):
            at = slice(16 * pair, 16 * pair + 16)

            def store_x(cp, p, block, at=at, rp=rp):
                xq_ref[rp, cp, p, at] = block

            def store_g(cp, p, block, at=at, rp=rp):
                for g in range(GROUPS):
                    g_ref[rp, g, cp, p, at] = block[:, 128 * g:128 * g + 128]

            to_patches([x_ref[2 * pair + d, rp] for d in range(2)], split_ref, store_x)
            to_patches([do_ref[2 * pair + d, rp] for d in range(2)], split_ref, store_g)
        for cp in range(2):
            qs = dot(xq_ref[rp, cp].reshape(256, 384), w_ref[:, :384]).astype(BF)
            for g in range(GROUPS):
                q_ref[rp, g, cp] = qs[:, 128 * g:128 * g + 128].reshape(8, 32, 128)


def window_bias(bias, key_rows, row_ok):
    shape = (16 * key_rows, 128)
    key = lax.broadcasted_iota(jnp.int32, shape, 0)
    lane = lax.broadcasted_iota(jnp.int32, shape, 1)
    krow, kcol = key // 16, key % 16
    qrow, dcol = (lane % 32) // 8, key % 16 - lane % 8
    ok = row_ok(krow, qrow) & (dcol >= 0) & (dcol <= 6)
    for which, extra in enumerate((kcol >= 3, kcol >= 0, kcol < 11)):
        bias[which] = jnp.where(ok & extra, 0.0, -1e30).astype(F32)


def head_masks():
    head_lane = lax.broadcasted_iota(jnp.int32, (32, 128), 1) // 32
    return [head_lane == h for h in range(4)], [(head_lane == h).astype(F32).astype(BF) for h in range(4)]


def pack_heads(rhs, slot, qp, gp, pick_b):
    for h in range(4):
        rhs[slot, 32 * h:32 * h + 32, :128] = qp * pick_b[h]
        rhs[slot, 128 + 32 * h:160 + 32 * h, 128:] = gp * pick_b[h]


def clear_off_diagonal(rhs):
    for slot in range(rhs.shape[0]):
        rhs[slot, :128, 128:] = jnp.zeros((128, 128), BF)
        rhs[slot, 128:, :128] = jnp.zeros((128, 128), BF)


def edge_kind(p):
    return 0 if p == 0 else (2 if p == 7 else 1)


def attend_kernel(rp, near_ref, far_ref, q, do, xq, kv, xk, w_ref, place_ref, *refs):
    if rp == 0:
        send_ref, gs_ref, *refs = refs
        gs_ref[:768] = send_ref[...].reshape(768, 384)
    dq_ref, own_ref, stat_ref, dw_ref, xh, kvh, acc, bias, wkv, sc, pd, rhs, tail = refs
    index = lax.axis_index("row")
    odd = index & 1
    low = jnp.where(index == 0, 3, 0)
    high = jnp.where(index == lax.axis_size("row") - 1, 7, 10)
    gather_kv_weight(w_ref, wkv)
    window_bias(bias, 10, lambda krow, qrow: (krow >= qrow) & (krow <= qrow + 6) & (krow >= low) & (krow < high))

    for k in range(3):
        project_keys(near_ref[0, k, rp], place_ref, wkv, xh, kvh, k + 3 - 3 * odd)
    for k in range(3):
        project_keys(far_ref[k], place_ref, wkv, xh, kvh, k + 3 * odd)
    pick, pick_b = head_masks()
    clear_off_diagonal(rhs)

    def attend(step, carry):
        def place_of(u):
            index = step * (UNITS // 8) + u // 8
            return index // 2, (u // 8) % 2, u % 8

        def keys(u):
            g, cp, p = place_of(u)
            return jnp.concatenate([
                kvh[g, cp, p, :3].reshape(48, 256),
                kv[rp, g, cp, p].reshape(64, 256),
                kvh[g, cp, p, 3:].reshape(48, 256)], axis=0)

        def score(u):
            g, cp, p = place_of(u)
            pack_heads(rhs, u % SLOTS, q[rp, g, cp, p], do[rp, g, cp, p], pick_b)
            sc[u % (LAG + 1)] = dot(keys(u), rhs[u % SLOTS], 1, 1)

        def soften(u):
            g, cp, p = place_of(u)
            now, slot = u % (LAG + 1), u % (LAG + 1)
            s = sc[now, :, :128] + bias[edge_kind(p)]
            m = jnp.max(s, axis=0, keepdims=True)
            e = jnp.exp2((s - m) * C)
            dp = sc[now, :, 128:]
            total = jnp.sum(e, axis=0, keepdims=True)
            inv = 1.0 / total
            delta = jnp.sum(e * dp, axis=0, keepdims=True) * inv
            att = e * inv
            pd[slot, :, :128] = (att * (dp - delta)).astype(BF)
            pd[slot, :, 128:] = att.astype(BF)
            stat_ref[0, g, cp, p:p + 1] = m * C + jnp.log2(total)
            stat_ref[1, g, cp, p:p + 1] = delta

        def spread(u):
            g, cp, p = place_of(u)
            slot = u % (LAG + 1)

            def add_to(at, value):
                acc[g, cp, :3, at, :] = value[:3]
                own_ref[g, cp, :, at, :] = value[3:7]
                acc[g, cp, 3:, at, :] = value[7:]

            dkv = dot(pd[slot], rhs[u % SLOTS]).reshape(10, 16, 256)
            head = dkv[:, :8]
            if p > 0:
                head = head + tail[(p + 1) % 2]
            add_to(slice(8 * p, 8 * p + 8), head)
            if p < 7:
                tail[p % 2] = dkv[:, 8:]
            else:
                add_to(slice(64, 72), dkv[:, 8:])
                add_to(slice(72, 80), jnp.zeros((10, 8, 256), F32))
            full = dot(pd[slot, :, :128], keys(u)[:, :128], 0, 0)
            dq = jnp.where(pick[3], full[96:], 0.0)
            for h in range(3):
                dq = jnp.where(pick[h], full[32 * h:32 * h + 32], dq)
            dq_ref[g, cp, p] = (dq * SCALE).astype(BF)

        for t in range(UNITS + 2 * LAG):
            if t < UNITS:
                score(t)
            if 0 <= t - LAG < UNITS:
                soften(t - LAG)
            if 0 <= t - 2 * LAG < UNITS:
                spread(t - 2 * LAG)
        return carry

    if UNITS == 48:
        attend(0, 0)
    else:
        lax.fori_loop(0, 48 // UNITS, attend, 0)
    if rp == 0:
        rest = stat_ref[...].reshape(96, 128)
        for part in range(3):
            piece = rest.astype(BF)
            gs_ref[768:, 128 * part:128 * part + 128] = piece
            rest = rest - piece.astype(F32)

    dw = jnp.zeros((384, 768), F32)
    dwq = jnp.zeros((384, 384), F32)
    for cp in range(2):
        for xs, ref, n in ((xh[cp], acc, 480), (xk[rp, cp], own_ref, 320)):
            parts = []
            for g in range(GROUPS):
                a = ref[g, cp].reshape(n, 256)
                parts.append((a[:, :128] * SCALE).astype(BF))
                parts.append(a[:, 128:].astype(BF))
            dw = dw + dot(xs.reshape(n, 384), jnp.concatenate(parts, axis=1), 0, 0)
        dqs = jnp.concatenate([dq_ref[g, cp].reshape(256, 128) for g in range(GROUPS)], axis=1)
        dwq = dwq + dot(xq[rp, cp].reshape(256, 384), dqs, 0, 0)

    dw_ref[:, :384] = dwq
    for g in range(GROUPS):
        dw_ref[:, 384 + 128 * g:512 + 128 * g] = dw[:, 256 * g:256 * g + 128]
        dw_ref[:, 768 + 128 * g:896 + 128 * g] = dw[:, 256 * g + 128:256 * g + 256]


def cross_kernel(rp, near_ref, far_ref, far_gs_ref, near_stat, far_stat, kv, own_ref, w_ref, split_ref,
                 dkvs, xq, q, do, bias, sc, pd, rhs, acc, tail, stats):
    odd = lax.axis_index("row") & 1
    if far_stat is None:
        parts = far_gs_ref[768:].astype(F32)
        far_rows = (parts[:, :128] + parts[:, 128:256] + parts[:, 256:]).reshape(near_stat.shape)
    else:
        far_rows = far_stat[...]
    stats[:, :, :, :, :128] = jnp.where(odd == 1, near_stat[...], far_rows)
    stats[:, :, :, :, 128:] = jnp.where(odd == 1, far_rows, near_stat[...])
    key = lax.broadcasted_iota(jnp.int32, (64, 256), 0)
    lane = lax.broadcasted_iota(jnp.int32, (64, 256), 1)
    krow, kcol, qrow = key // 16, key % 16, (lane % 32) // 8
    dcol = kcol - lane % 8
    ok = ((lane < 128) & (krow < qrow)) | ((lane >= 128) & (krow > qrow))
    ok = ok & (dcol >= 0) & (dcol <= 6)
    for which, extra in enumerate((kcol >= 3, kcol >= 0, kcol < 11)):
        bias[which] = jnp.where(ok & extra, 0.0, -1e30).astype(F32)
    pick, pick_b = head_masks()

    def side_patches(side, x_row, d_row):
        lines = [None, 0, 1, 2] if side == 0 else [0, 1, 2, None]
        for pair in range(2):
            rows = lines[2 * pair:2 * pair + 2]
            at = slice(16 * pair, 16 * pair + 16)

            def store_x(cp, p, block, at=at):
                xq[cp, p, at] = block

            def store_g(cp, p, block, at=at):
                for g in range(GROUPS):
                    do[side, g, cp, p, at] = block[:, 128 * g:128 * g + 128]

            to_patches([None if r is None else x_row(r) for r in rows], split_ref, store_x)
            to_patches([None if r is None else d_row(r) for r in rows], split_ref, store_g)
        for cp in range(2):
            qs = dot(xq[cp].reshape(256, 384), w_ref[:, :384]).astype(BF)
            for g in range(GROUPS):
                q[side, g, cp] = qs[:, 128 * g:128 * g + 128].reshape(8, 32, 128)

    for parity in range(2):
        @pl.when(odd == parity)
        def _(parity=parity):
            side_patches(1 - parity, lambda r: near_ref[0, r, rp], lambda r: near_ref[1, r, rp])
            side_patches(parity, lambda r: far_ref[r], lambda r: far_gs_ref[256 * r + 128 * rp:256 * r + 128 * rp + 128])

    def attend(step, carry):
        def place_of(u):
            index = step * (CROSS_UNITS // 8) + u // 8
            return index // 2, (u // 8) % 2, u % 8

        def score(u):
            g, cp, p = place_of(u)
            slot = u % SLOTS
            for side in range(2):
                for h in range(4):
                    at = slice(128 * side + 32 * h, 128 * side + 32 * h + 32)
                    rhs[slot, 0, at] = q[side, g, cp, p] * pick_b[h]
                    rhs[slot, 1, at] = do[side, g, cp, p] * pick_b[h]
            keys = kv[rp, g, cp, p].reshape(64, 256)
            for part in range(2):
                sc[u % (LAG + 1), part] = dot(keys[:, 128 * part:128 * part + 128], rhs[slot, part], 1, 1)

        def soften(u):
            g, cp, p = place_of(u)
            now = u % (LAG + 1)
            s = (sc[now, 0] + bias[edge_kind(p)]) * C
            att = jnp.exp2(s - stats[0, g, cp, p:p + 1])
            pd[now, 0] = (att * (sc[now, 1] - stats[1, g, cp, p:p + 1])).astype(BF)
            pd[now, 1] = att.astype(BF)

        def spread(u):
            g, cp, p = place_of(u)
            for part in range(2):
                lanes = slice(128 * part, 128 * part + 128)
                value = dot(pd[u % (LAG + 1), part], rhs[u % SLOTS, part]).reshape(4, 16, 128)
                head = value[:, :8] + own_ref[g, cp, :, 8 * p:8 * p + 8, lanes]
                if p > 0:
                    head = head + tail[(p + 1) % 2, :, :, lanes]
                acc[:, 8 * p:8 * p + 8, lanes] = head
                if p < 7:
                    tail[p % 2, :, :, lanes] = value[:, 8:]
                else:
                    acc[:, 64:72, lanes] = value[:, 8:] + own_ref[g, cp, :, 64:72, lanes]
            if p == 7:
                acc[:, 72:80, :] = jnp.zeros((4, 8, 256), F32)
                dkvs[g, cp, :, :, :128] = (acc[:, :, :128] * SCALE).astype(BF)
                dkvs[g, cp, :, :, 128:] = acc[:, :, 128:].astype(BF)

        for t in range(CROSS_UNITS + 2 * LAG):
            if t < CROSS_UNITS:
                score(t)
            if 0 <= t - LAG < CROSS_UNITS:
                soften(t - LAG)
            if 0 <= t - 2 * LAG < CROSS_UNITS:
                spread(t - 2 * LAG)
        return carry

    if CROSS_UNITS == 48:
        attend(0, 0)
    else:
        lax.fori_loop(0, 48 // CROSS_UNITS, attend, 0)


def final_kernel(dq0_ref, dq1_ref, dkv0_ref, dkv1_ref, w_ref, unplace_ref, unsplit_ref, out_ref):
    for rp, (dq_ref, dkvs) in enumerate(((dq0_ref, dkv0_ref), (dq1_ref, dkv1_ref))):
        for pair in range(2):
            quads = [jnp.concatenate([dq_ref[g, cp, p, 16 * pair:16 * pair + 16] for g in range(GROUPS)], axis=1).astype(F32)
                     for cp in range(2) for p in range(8)]
            for sub in range(2):
                kq = 2 * pair + sub
                dqs = jnp.concatenate([t[8 * sub:8 * sub + 8] for t in quads], axis=0).astype(BF)
                parts = [jnp.concatenate([dkvs[g, 0, kq], dkvs[g, 1, kq]], axis=0) for g in range(GROUPS)]
                both = jnp.concatenate([t[:, :128] for t in parts] + [t[:, 128:] for t in parts], axis=1)
                nq = dot(unsplit_ref[...], dqs).astype(BF)
                nkv = dot(unplace_ref[...], both).astype(BF)
                out_ref[2 * kq + rp] = dot(jnp.concatenate([nq, nkv], axis=1), w_ref[...], 1, 1).astype(BF)


def after(value, *others):
    return lax.optimization_barrier((value,) + others)[0]


def exchange(x, axis, dim, bit_count, low, behind):
    count = lax.axis_size(axis)
    span = 1 << bit_count
    mine = (lax.axis_index(axis) >> low) & (span - 1)
    total = lax.dynamic_index_in_dim(x, mine, dim, keepdims=False).astype(F32)
    sent = [lax.ppermute(lax.dynamic_index_in_dim(x, mine ^ turn, dim, keepdims=False).astype(BF), axis,
                         [(i, i ^ (turn << low)) for i in range(count)]) for turn in range(1, span)]
    for block in lax.optimization_barrier((behind, *sent))[1:]:
        total = total + block.astype(F32)
    return total


VM = pl.BlockSpec(memory_space=pltpu.VMEM)
ANY = pl.BlockSpec(memory_space=pl.ANY)


def call(kernel, name, us, outs, scratch, args):
    return pl.pallas_call(
        kernel,
        out_shape=[jax.ShapeDtypeStruct(s, t) for s, t in outs],
        in_specs=[VM] * len(args),
        out_specs=[VM] * len(outs),
        scratch_shapes=[pltpu.VMEM(s, t) for s, t in scratch],
        compiler_params=pltpu.CompilerParams(vmem_limit_bytes=VMEM_BYTES),
        cost_estimate=pl.CostEstimate(flops=int(us * 1e9), bytes_accessed=1 << 20, transcendentals=0),
        name=name,
    )(*args)


def raw_call(kernel, name, outs, scratch, args):
    return pl.pallas_call(
        kernel,
        out_shape=[jax.ShapeDtypeStruct(s, BF) for s in outs],
        in_specs=[ANY] * len(args),
        out_specs=[ANY] * len(outs),
        scratch_shapes=[pltpu.VMEM(s, BF) for s in scratch] + [pltpu.SemaphoreType.DMA((10,))],
        name=name,
    )(*args)


def own_call(*args):
    outs = [(2, 3, 2, 8, 32, 128), (2, 3, 2, 8, 32, 128), (2, 2, 8, 32, 384), (2, 3, 2, 8, 4, 16, 256), (2, 2, 4, 80, 384)]
    return pl.pallas_call(
        own_kernel,
        out_shape=[jax.ShapeDtypeStruct(s, BF) for s in outs],
        in_specs=[ANY] * len(args),
        out_specs=[VM] * len(outs),
        scratch_shapes=[pltpu.VMEM((384, 768), BF)] + [pltpu.VMEM(a.shape, BF) for a in args] + [pltpu.SemaphoreType.DMA((5,))],
        compiler_params=pltpu.CompilerParams(vmem_limit_bytes=VMEM_BYTES),
        cost_estimate=pl.CostEstimate(flops=4000000000, bytes_accessed=1 << 20, transcendentals=0),
        name="own",
    )(*args)


def attend_call(rp, *args):
    def kernel(*refs):
        attend_kernel(rp, *refs)

    outs = [((3, 2, 8, 32, 128), BF), ((3, 2, 4, 80, 256), F32), ((2, 3, 2, 8, 128), F32), ((384, 1152), F32)]
    if rp == 0:
        outs = [((864, 384), BF)] + outs
    return call(kernel, "attend", 10, outs, [
        ((2, 6, 80, 384), BF), ((3, 2, 8, 6, 16, 256), BF), ((3, 2, 6, 80, 256), F32), ((3, 160, 128), F32),
        ((384, 768), BF), ((LAG + 1, 160, 256), F32), ((LAG + 1, 160, 256), BF), ((SLOTS, 256, 256), BF), ((2, 10, 8, 256), F32),
    ], args)


def cross_call(rp, near, far, far_gs, stat_near, stat_far, kv, own, w, split):
    args = [near, far, far_gs, stat_near, stat_far, kv, own, w, split]
    if rp == 0:
        del args[4]

    def kernel(*refs):
        refs = list(refs)
        if rp == 0:
            refs.insert(4, None)
        cross_kernel(rp, *refs)

    return call(kernel, "cross", 6, [((3, 2, 4, 80, 256), BF)], [
        ((2, 8, 32, 384), BF), ((2, 3, 2, 8, 32, 128), BF), ((2, 3, 2, 8, 32, 128), BF),
        ((3, 64, 256), F32), ((LAG + 1, 2, 64, 256), F32), ((LAG + 1, 2, 64, 256), BF), ((SLOTS, 2, 256, 128), BF),
        ((4, 80, 256), F32), ((2, 4, 8, 256), F32), ((2, 3, 2, 8, 256), F32),
    ], args)[0]


def final_call(shape, *args):
    return call(final_kernel, "final", 4, [(shape, BF)], [], args)[0]


def shards(features, qkv_weight, grad_output):
    row_count, col_count, width = features.shape
    count = lax.axis_size("row")
    near = [(i, i ^ 1) for i in range(count)]
    far = [(i, i + 1) for i in range(1, count - 1, 2)] + [(i + 1, i) for i in range(1, count - 1, 2)]
    place, split = column_maps()
    x4, g4 = (a.reshape(row_count // 2, 2, col_count, width) for a in (features, grad_output))
    rim = (col_count, width)
    sends = [(3,) + rim, (2, 3, 2) + rim, (3,) + rim, (3, 2) + rim]
    send_x0, send_near, send_x1, send_g = raw_call(pack_kernel, "pack", sends, sends, (x4, g4))
    far_x0 = lax.ppermute(send_x0, "row", far)
    near_xg = lax.ppermute(send_near, "row", near)
    q, do, xq, kv, xk = own_call(x4, g4, qkv_weight, place, split)
    far_x1 = lax.ppermute(after(send_x1, far_x0, xk), "row", far)
    gs, dq0, own0, stat0, dw0 = attend_call(0, near_xg, far_x0, q, do, xq, kv, xk, qkv_weight, place, send_g)
    far_x1 = after(far_x1, dw0)
    far_gs = lax.ppermute(after(gs, far_x1), "row", far)
    stat0_near = lax.ppermute(stat0, "row", near)
    dq1, own1, stat1, dw1 = attend_call(1, near_xg, far_x1, q, do, xq, kv, xk, qkv_weight, place)
    far_gs, stat0_near, _ = lax.optimization_barrier((far_gs, stat0_near, dq1))
    stat1_near = lax.ppermute(stat1, "row", near)
    stat1_far = lax.ppermute(stat1, "row", far)
    bits = count.bit_length() - 1
    rows = width // count
    dkv0 = cross_call(0, near_xg, far_x0, far_gs, stat0_near, None, kv, own0, qkv_weight, split)
    stat1_near, stat1_far, _ = lax.optimization_barrier((stat1_near, stat1_far, dkv0))
    total = exchange((dw0 + dw1).reshape(count // 2, 2, rows, 3 * width), "row", 1, 1, 0, dkv0)
    dkv1 = cross_call(1, near_xg, far_x1, far_gs, stat1_near, stat1_far, kv, own1, qkv_weight, split)
    total = exchange(total.reshape(count // 4, 2, rows, 3 * width), "row", 1, 1, 1, dkv1)
    grad_features = final_call(features.shape, dq0, dq1, dkv0, dkv1, qkv_weight, place.T, split.T)
    low = 2
    while low < bits:
        step = min(2, bits - low)
        total = exchange(total.reshape(count >> (low + step), 1 << step, rows, 3 * width), "row", 1, step, low, grad_features)
        low += step
    grad_weight = total.reshape(rows, 3 * width) * (row_count * count * col_count) ** -0.5
    return grad_features, grad_weight


def solution(mesh):
    placed = (P(("group", "row"), None, None), P(), P(("group", "row"), None, None))
    return jax.shard_map(
        shards,
        mesh=mesh,
        in_specs=placed,
        out_specs=(P(("group", "row"), None, None), P(("group", "row"), None)),
        check_vma=False,
    )
```
